256 devices in a mesh: view: 16 (over z, y_hi), tok: 16 (over y_lo, x, core).
Axes of the slice: x: 4, y: 4 (y_hi: 2, y_lo: 2; y = y_hi * 2 + y_lo), z: 8, core: 2. Of those that a mesh axis runs over, the one named last changes fastest.
Arguments:
- q1: bfloat16 [16, 512, 1024], P('view', 'tok'), may hold values from -96 to 96
- k1: bfloat16 [16, 512, 1024], P('view', 'tok'), may hold values from -6 to 6
- v1: bfloat16 [16, 512, 1024], P('view', 'tok'), may hold values from -6 to 6
- nbr: int32 [16, 7], P('view'), may hold values from 0 to 15, as said below
- x2: bfloat16 [16, 512, 1024], P('view', 'tok'), may hold values from -6 to 6
- w_view_out: bfloat16 [1024, 1024], replicated, may hold values from -0.1875 to 0.1875
- norm_gain: float32 [1024], replicated, may hold values from 0.5 to 1.5
- w_qkv: bfloat16 [1024, 3072], replicated, may hold values from -0.1875 to 0.1875
- w_out: bfloat16 [1024, 1024], replicated, may hold values from -0.1875 to 0.1875
Outputs:
- view_feats: float32 [16, 512, 1024], P('view', 'tok')
- lrm_out: float32 [16, 512, 1024], P('view', 'tok')
The draws below stay inside these ranges and needn't reach their ends.
Inputs may be any that keep to these rules, and one draw needn't show every extreme that they name: `nbr`: row v lists 7 distinct view indices, none equal to v.
All inputs are finite; a program needn't handle non-finite values.
Results may differ from the reference program's by a relative error of at most 0.014.
Values may be sent and summed in bfloat16 or wider, within the bound.
A program may use at most 128 MiB of HBM per device.

```python
import jax
import jax.numpy as jnp
from jax import lax

H1 = 16
HD1 = 64
NBR = 7
H2 = 16
HD2 = 64
VIEWS = 16
TOKV = 512
F1 = 1024
D2 = 1024


def paired_draw(key):
    shape = (VIEWS, TOKV, F1)
    keys_part = jnp.clip(jax.random.normal(jax.random.fold_in(key, 11), shape, jnp.float32), -6.0, 6.0)
    query_part = jnp.clip(jax.random.normal(jax.random.fold_in(key, 12), shape, jnp.float32), -6.0, 6.0)
    return (query_part, keys_part)


def draw_q1(key, part):
    return paired_draw(key)[0].astype(jnp.bfloat16)


def draw_k1(key, part):
    return paired_draw(key)[1].astype(jnp.bfloat16)


def draw_nbr(key, part):
    split_keys = jax.random.split(key, VIEWS)
    offsets = jax.vmap(lambda one_key: jax.random.permutation(one_key, VIEWS - 1)[:NBR])(split_keys)
    return ((jnp.arange(VIEWS)[:, None] + 1 + offsets) % VIEWS).astype(jnp.int32)


def level_of(own_key, dims, cuts, low, largest):
    loudness, own = 1.0, jax.random.fold_in(own_key, 6)
    for axis_at, shards_of in cuts:
        draws = jnp.exp(jax.random.uniform(jax.random.fold_in(own, axis_at), (shards_of,), jnp.float32, low / len(cuts), largest / len(cuts)))
        loudness = loudness * jnp.repeat(draws, dims[axis_at] // shards_of).reshape([-1 if axis == axis_at else 1 for axis in range(len(dims))])
    return loudness


def noise(key, dims, scale, most, pieces=(), kind=jnp.bfloat16):
    values = scale * jax.random.normal(key, dims, jnp.float32)
    if pieces:
        values = values * level_of(key, dims, pieces, -0.22, 0.18)
    return jnp.clip(values, -most, most).astype(kind)


def setup_inputs(seed: int = 0) -> dict:
    splits = jax.random.split(jax.random.key(seed), 10)
    return {
        "q1": draw_q1(jax.random.fold_in(splits[9], 71), 0),
        "k1": draw_k1(jax.random.fold_in(splits[9], 71), 0),
        "v1": noise(splits[2], (VIEWS, TOKV, F1), 1.0, 6.0, ((0, 16), (1, 16))),
        "nbr": draw_nbr(jax.random.fold_in(splits[9], 71), 0),
        "x2": noise(splits[4], (VIEWS, TOKV, D2), 1.0, 6.0, ((0, 16), (1, 16))),
        "w_view_out": noise(splits[5], (F1, D2), F1 ** -0.5, 0.1875),
        "norm_gain": jnp.clip(1.0 + 0.1 * jax.random.normal(splits[6], (D2,), jnp.float32), 0.5, 1.5),
        "w_qkv": noise(splits[7], (D2, 3 * D2), D2 ** -0.5, 0.1875),
        "w_out": noise(splits[8], (D2, D2), D2 ** -0.5, 0.1875),
    }


EPSILON = 1e-06

def reference(q1, k1, v1, nbr, x2, w_view_out, norm_gain, w_qkv, w_out):
    scale_one = HD1 ** (-0.5)
    scale_two = HD2 ** (-0.5)

    def one_view(view_id):
        chosen = jnp.concatenate([jnp.reshape(view_id, (1,)).astype(jnp.int32), nbr[view_id].astype(jnp.int32)])
        keys = k1[chosen].reshape(-1, H1, HD1).astype(jnp.float32)
        values = v1[chosen].reshape(-1, H1, HD1).astype(jnp.float32)
        queries = q1[view_id].reshape(TOKV, H1, HD1).astype(jnp.float32)
        scores = jnp.einsum('qhd,khd->qhk', queries, keys) * scale_one
        peak = lax.optimization_barrier(jnp.max(scores, axis=-1, keepdims=True))
        weights = jnp.exp(scores - peak)
        row_total = lax.optimization_barrier(jnp.sum(weights, axis=-1))
        rounded = lax.optimization_barrier(weights.astype(jnp.bfloat16)).astype(jnp.float32)
        summed = jnp.einsum('qhk,khd->qhd', rounded, values)
        attn = (summed / row_total[..., None]).reshape(TOKV, F1)
        return attn * lax.rsqrt(lax.optimization_barrier(jnp.mean(attn * attn, axis=-1, keepdims=True)) + EPSILON)
    features = lax.map(one_view, jnp.arange(VIEWS, dtype=jnp.int32))
    flat = features.reshape(VIEWS * TOKV, F1).astype(jnp.bfloat16)
    hidden = x2.reshape(VIEWS * TOKV, D2).astype(jnp.float32) + jnp.dot(flat, w_view_out, preferred_element_type=jnp.float32)
    normed = (hidden * lax.rsqrt(lax.optimization_barrier(jnp.mean(hidden * hidden, axis=-1, keepdims=True)) + EPSILON) * norm_gain).astype(jnp.bfloat16)
    projected = jnp.dot(normed, w_qkv, preferred_element_type=jnp.float32).astype(jnp.bfloat16)
    projected = projected.reshape(VIEWS * TOKV, 3, H2, HD2)
    all_q = projected[:, 0].reshape(VIEWS, TOKV, H2, HD2)
    all_k = projected[:, 1]
    all_v = projected[:, 2]

    def one_head(head):
        keys = all_k[:, head]
        values = all_v[:, head]

        def one_block(block):
            queries = all_q[block, :, head]
            scores = jnp.dot(queries, keys.T, preferred_element_type=jnp.float32) * scale_two
            peak = lax.optimization_barrier(jnp.max(scores, axis=-1, keepdims=True))
            weights = jnp.exp(scores - peak)
            row_total = lax.optimization_barrier(jnp.sum(weights, axis=-1, keepdims=True))
            summed = jnp.dot(weights.astype(jnp.bfloat16), values, preferred_element_type=jnp.float32)
            return summed / row_total
        return lax.map(one_block, jnp.arange(VIEWS, dtype=jnp.int32))
    heads = lax.map(one_head, jnp.arange(H2, dtype=jnp.int32))
    attn_two = jnp.transpose(heads, (1, 2, 0, 3)).reshape(VIEWS * TOKV, D2).astype(jnp.bfloat16)
    wide = attn_two.astype(jnp.float32)
    unit_rows = (wide * lax.rsqrt(lax.optimization_barrier(jnp.mean(wide * wide, axis=-1, keepdims=True)) + EPSILON)).astype(jnp.bfloat16)
    result = jnp.dot(unit_rows, w_out, preferred_element_type=jnp.float32)
    return (features, result.reshape(VIEWS, TOKV, D2))
```

```python
import math

import jax
import jax.numpy as jnp
from jax import lax
from jax.experimental import pallas as pl
from jax.experimental.pallas import tpu as pltpu
from jax.sharding import PartitionSpec as P

MESH = pl.DeviceIdType.MESH
BF = jnp.bfloat16
F32 = jnp.float32

EPSILON = 1e-06
NEGATIVE = -1e30
START_MAX = -3e38
HD = 64
LANES = 2 * HD
Z = 8
HEADS = 16
TOKS = 16
MY_ROWS = 32
WIDTH = HEADS * HD
ROWS = TOKS * MY_ROWS
VIEWS = 2 * Z
SUB = 4
PIECE = ROWS // SUB
EXP2_SCALE = HD ** (-0.5) * math.log2(math.e)


def wait_bytes(like, sem):
    pltpu.make_async_copy(like, like, sem).wait()


def rows_of(ref, start, count):
    return ref.at[pl.ds(pl.multiple_of(start, count if count < 128 else 128), count), :]


def pack(q_of, k_of, v_of, extra, sq, skv):
    low = lax.broadcasted_iota(jnp.int32, (MY_ROWS, LANES), 1) < HD
    for pair in range(HEADS // 2):
        q, k, v = q_of(pair), k_of(pair), v_of(pair)
        turned_q, turned_k, turned_v = (pltpu.roll(part, HD, 1) for part in (q, k, v))
        first, second = 2 * pair * MY_ROWS, (2 * pair + 1) * MY_ROWS
        sq[first : first + MY_ROWS, :] = jnp.where(low, q, extra).astype(BF)
        sq[second : second + MY_ROWS, :] = jnp.where(low, turned_q, extra).astype(BF)
        skv[first : first + MY_ROWS, :] = jnp.where(low, k, turned_v).astype(BF)
        skv[second : second + MY_ROWS, :] = jnp.where(low, turned_k, v).astype(BF)


def kernel(
    nbr, q1, k1, v1, x2, w_view_out, norm_gain, w_qkv, w_out,
    feats_out, lrm_out,
    q_in, k_in, v_in, x_in, gain_in, wv, wqkv, wo,
    sq_one, skv_one, qb_one, kv_one, so_one, ro_one,
    sq_two, skv_two, qb_two, kv_two, so_two, ro_two,
    peak, acc, feats, result,
    load_sem, weight_sem, out_sem, a2a_send, a2a_q, a2a_kv, ring_send, ring_recv, pair_send, pair_recv, back_send, back_recv,
):
    view = lax.axis_index("view")
    tok = lax.axis_index("tok")
    z, y_hi = view // 2, view % 2
    core = tok % 2
    my_head = y_hi * 8 + tok // 8 * 4 + tok // 2 % 4
    my_view = z * 2 + core
    at_home = core == y_hi
    right = (z + 1) % Z * 2 + y_hi
    left = (z + Z - 1) % Z * 2 + y_hi
    partner = tok + 1 - 2 * core

    loads = [
        pltpu.make_async_copy(src, dst, load_sem.at[i])
        for i, (src, dst) in enumerate(
            ((q1.at[0], q_in), (k1.at[0], k_in), (v1.at[0], v_in), (x2.at[0], x_in), (norm_gain, gain_in))
        )
    ]
    weights = [
        pltpu.make_async_copy(src, dst, weight_sem.at[i])
        for i, (src, dst) in enumerate(((w_view_out, wv), (w_qkv, wqkv), (w_out, wo)))
    ]
    for copy in loads:
        copy.start()

    def head_device(head):
        return (z * 2 + head // 8, head // 4 % 2 * 8 + head % 4 * 2 + y_hi)

    def row_device(member):
        return (my_view, member)

    barrier = pltpu.get_barrier_semaphore()

    def greet(i, _):
        head_view, head_tok = head_device(i)

        @pl.when(jnp.logical_or(head_view != view, head_tok != tok))
        def _():
            pl.semaphore_signal(barrier, inc=1, device_id=(head_view, head_tok), device_id_type=MESH)

        @pl.when(jnp.logical_or(my_view != view, i != tok))
        def _():
            pl.semaphore_signal(barrier, inc=1, device_id=(my_view, i), device_id_type=MESH)

        return 0

    lax.fori_loop(0, TOKS, greet, 0)
    pl.semaphore_signal(barrier, inc=1, device_id=(right, tok), device_id_type=MESH)
    pl.semaphore_signal(barrier, inc=1, device_id=(left, tok), device_id_type=MESH)
    pl.semaphore_signal(barrier, inc=1, device_id=(view, partner), device_id_type=MESH)

    for copy in weights:
        copy.start()

    lane = lax.broadcasted_iota(jnp.int32, (1, LANES), 1)
    low_ones = jnp.where(lane < HD, 1.0, 0.0).astype(BF)
    high_ones = jnp.where(lane < HD, 0.0, 1.0).astype(BF)

    def all_to_all(stage, sq, skv, qb, kv):
        def send(i, _):
            head = (my_head + i) % HEADS
            head_view, head_tok = head_device(head)
            mine = jnp.logical_and(head_view == view, head_tok == tok)
            src_q = rows_of(sq, head * MY_ROWS, MY_ROWS)
            dst_q = rows_of(qb, tok * MY_ROWS, MY_ROWS)
            src_kv = rows_of(skv, head * MY_ROWS, MY_ROWS)
            dst_kv = rows_of(kv, view * ROWS + tok * MY_ROWS, MY_ROWS)
            sem_kv = a2a_kv.at[stage, tok * MY_ROWS // PIECE]

            @pl.when(mine)
            def _():
                pltpu.make_async_copy(src_kv, dst_kv, sem_kv).start()
                pltpu.make_async_copy(src_q, dst_q, a2a_q.at[stage]).start()

            @pl.when(jnp.logical_not(mine))
            def _():
                for src, dst, sem, k in ((src_kv, dst_kv, sem_kv, 0), (src_q, dst_q, a2a_q.at[stage], 1)):
                    pltpu.make_async_remote_copy(
                        src_ref=src,
                        dst_ref=dst,
                        send_sem=a2a_send.at[stage, k],
                        recv_sem=sem,
                        device_id=(head_view, head_tok),
                        device_id_type=MESH,
                    ).start()

            return 0

        lax.fori_loop(0, HEADS, send, 0)

    def sent(like, sem):
        @pl.when(at_home)
        def _():
            wait_bytes(like.at[pl.ds(0, (HEADS - 1) * MY_ROWS), :], sem)

        @pl.when(jnp.logical_not(at_home))
        def _():
            wait_bytes(like.at[pl.ds(0, HEADS * MY_ROWS), :], sem)

    def ring_piece(stage, kv, direction, step, sub):
        from_z = (z + Z - step) % Z if direction == 0 else (z + step) % Z
        block = rows_of(kv, (from_z * 2 + core) * ROWS + sub * PIECE, PIECE)
        pltpu.make_async_remote_copy(
            src_ref=block,
            dst_ref=block,
            send_sem=ring_send.at[stage, direction],
            recv_sem=ring_recv.at[stage, direction, step * SUB + sub],
            device_id=(right if direction == 0 else left, tok),
            device_id_type=MESH,
        ).start()

    def to_partner(stage, kv, from_z, sub, slot):
        block = rows_of(kv, (from_z * 2 + core) * ROWS + sub * PIECE, PIECE)
        pltpu.make_async_remote_copy(
            src_ref=block,
            dst_ref=block,
            send_sem=pair_send.at[stage],
            recv_sem=pair_recv.at[stage, slot],
            device_id=(view, partner),
            device_id_type=MESH,
        ).start()

    def absorb(kv, qb, which, masked):
        block = kv[pl.ds(pl.multiple_of(which * ROWS, ROWS), ROWS), :]
        keys = block
        if masked:
            hot = jnp.where(lane == HD + which, 1.0, 0.0).astype(BF)
            keys = block * low_ones + hot
        values = block * high_ones + low_ones
        for half in range(2):
            cols = slice(half * (ROWS // 2), (half + 1) * (ROWS // 2))
            scores = lax.dot_general(
                keys, qb[cols, :], (((1,), (1,)), ((), ())), preferred_element_type=F32
            )
            old = peak[:, cols]
            new = jnp.maximum(old, jnp.max(scores, axis=0, keepdims=True))
            factor = jnp.exp2((old - new) * EXP2_SCALE)
            weights16 = jnp.exp2((scores - new) * EXP2_SCALE).astype(BF)
            part = lax.dot_general(
                values, weights16, (((0,), (0,)), ((), ())), preferred_element_type=F32
            )
            acc[:, cols] = acc[:, cols] * factor + part
            peak[:, cols] = new

    def attend(stage, qb, kv, masked):
        peak[...] = jnp.full_like(peak, START_MAX)
        acc[...] = jnp.zeros_like(acc)
        for sub in range(SUB):
            wait_bytes(rows_of(kv, my_view * ROWS + sub * PIECE, PIECE), a2a_kv.at[stage, sub])
            ring_piece(stage, kv, 0, 0, sub)
            ring_piece(stage, kv, 1, 0, sub)
            to_partner(stage, kv, z, sub, 0)
        wait_bytes(qb, a2a_q.at[stage])

        def piece_of(step, sub, direction):
            from_z = (z + Z - step) % Z if direction == 0 else (z + step) % Z
            slot = 2 * step - 1 + direction
            block = rows_of(kv, (from_z * 2 + core) * ROWS + sub * PIECE, PIECE)
            wait_bytes(block, ring_recv.at[stage, direction, (step - 1) * SUB + sub])
            if direction == 0:
                go_on = jnp.logical_or(step < Z // 2 - 1, sub < SUB // 2)
            else:
                go_on = jnp.logical_or(step < Z // 2 - 1, sub >= SUB // 2)

            @pl.when(jnp.logical_and(step < Z // 2, go_on))
            def _():
                ring_piece(stage, kv, direction, step, sub)

            to_partner(stage, kv, from_z, sub, jnp.minimum(slot, Z - 1))

        def step_of(i, _):
            step, sub = i // SUB + 1, i % SUB
            last = step == Z // 2

            @pl.when(jnp.logical_or(jnp.logical_not(last), sub < SUB // 2))
            def _():
                piece_of(step, sub, 0)

            @pl.when(jnp.logical_or(jnp.logical_not(last), sub >= SUB // 2))
            def _():
                piece_of(step, sub, 1)

            @pl.when(jnp.logical_or(step > 1, sub < 2))
            def _():
                direction, other = sub % 2, sub // 2
                first = step == 1
                behind = step - 1
                from_z = jnp.where(direction == 0, (z + Z - behind) % Z, (z + behind) % Z)
                use_other = jnp.where(first, sub, other)
                whose = core + use_other * (1 - 2 * core)
                which = jnp.where(first, z, from_z) * 2 + whose
                slot = jnp.where(first, 0, 2 * behind - 1 + direction)

                @pl.when(use_other == 1)
                def _():
                    wait_bytes(rows_of(kv, which * ROWS, ROWS), pair_recv.at[stage, slot])

                absorb(kv, qb, which, masked)

            return 0

        lax.fori_loop(0, Z // 2 * SUB, step_of, 0)
        far = (z + Z // 2) % Z * 2

        def last_two(i, _):
            which = far + core + i * (1 - 2 * core)

            @pl.when(i == 1)
            def _():
                wait_bytes(rows_of(kv, which * ROWS, ROWS), pair_recv.at[stage, Z - 1])

            absorb(kv, qb, which, masked)
            return 0

        lax.fori_loop(0, 2, last_two, 0)

    def ring_sent(stage, kv):
        for direction in range(2):
            wait_bytes(kv.at[pl.ds(0, ((Z // 2 - 1) * SUB + SUB // 2) * PIECE), :], ring_send.at[stage, direction])
        wait_bytes(kv.at[pl.ds(0, Z * ROWS), :], pair_send.at[stage])

    def send_back(stage, so, ro):
        whole = acc[...]
        so[...] = jnp.transpose(whole * (1.0 / whole[0:1, :])).astype(BF)

        def send(i, _):
            member = (tok + i) % TOKS
            mine = jnp.logical_and(my_view == view, member == tok)
            src = rows_of(so, member * MY_ROWS, MY_ROWS)
            dst = rows_of(ro, my_head * MY_ROWS, MY_ROWS)

            @pl.when(mine)
            def _():
                pltpu.make_async_copy(src, dst, back_recv.at[stage]).start()

            @pl.when(jnp.logical_not(mine))
            def _():
                pltpu.make_async_remote_copy(
                    src_ref=src,
                    dst_ref=dst,
                    send_sem=back_send.at[stage],
                    recv_sem=back_recv.at[stage],
                    device_id=(my_view, member),
                    device_id_type=MESH,
                ).start()

            return 0

        lax.fori_loop(0, TOKS, send, 0)
        wait_bytes(ro, back_recv.at[stage])

    def side_by_side(ro):
        low = lax.broadcasted_iota(jnp.int32, (MY_ROWS, LANES), 1) < HD
        parts = []
        for pair in range(HEADS // 2):
            first = ro[2 * pair * MY_ROWS : (2 * pair + 1) * MY_ROWS, :].astype(F32)
            second = ro[(2 * pair + 1) * MY_ROWS : (2 * pair + 2) * MY_ROWS, :].astype(F32)
            parts.append(jnp.where(low, pltpu.roll(first, HD, 1), second))
        return jnp.concatenate(parts, axis=1)

    def unit(values):
        return values * lax.rsqrt(jnp.mean(values * values, axis=-1, keepdims=True) + EPSILON)

    for copy in loads[:3]:
        copy.wait()
    lanes = lax.broadcasted_iota(jnp.int32, (MY_ROWS, LANES), 1)
    wanted = lanes == HD + view
    for i in range(nbr.shape[1]):
        wanted = jnp.logical_or(wanted, lanes == HD + nbr[0, i])
    bias = jnp.where(jnp.logical_or(wanted, lanes >= HD + VIEWS), 0.0, NEGATIVE)

    def cut(ref):
        return lambda pair: ref[:, pair * LANES : (pair + 1) * LANES].astype(F32)

    pack(cut(q_in), cut(k_in), cut(v_in), bias, sq_one, skv_one)
    pl.semaphore_wait(barrier, jnp.where(at_home, 2 * TOKS + 1, 2 * TOKS + 3))
    all_to_all(0, sq_one, skv_one, qb_one, kv_one)
    attend(0, qb_one, kv_one, True)
    send_back(0, so_one, ro_one)

    attn = side_by_side(ro_one)
    feats_f32 = unit(attn)
    feats[...] = feats_f32
    feats_copy = pltpu.make_async_copy(feats, feats_out.at[0], out_sem.at[0])
    feats_copy.start()
    for copy in loads[3:]:
        copy.wait()
    weights[0].wait()
    hidden = x_in[...].astype(F32) + jnp.dot(feats_f32.astype(BF), wv[...], preferred_element_type=F32)
    normed = (unit(hidden) * gain_in[...]).astype(BF)
    weights[1].wait()
    projected = [
        jnp.dot(normed, wqkv[:, part * WIDTH : (part + 1) * WIDTH], preferred_element_type=F32)
        for part in range(3)
    ]

    def cut_value(value):
        return lambda pair: value[:, pair * LANES : (pair + 1) * LANES]

    pack(*(cut_value(part) for part in projected), jnp.zeros((MY_ROWS, LANES), F32), sq_two, skv_two)

    all_to_all(1, sq_two, skv_two, qb_two, kv_two)
    attend(1, qb_two, kv_two, False)
    send_back(1, so_two, ro_two)
    unit_rows = unit(side_by_side(ro_two)).astype(BF)
    weights[2].wait()
    result[...] = jnp.dot(unit_rows, wo[...], preferred_element_type=F32)
    result_copy = pltpu.make_async_copy(result, lrm_out.at[0], out_sem.at[1])
    result_copy.start()

    for stage, (sq, skv, kv, so) in enumerate(
        ((sq_one, skv_one, kv_one, so_one), (sq_two, skv_two, kv_two, so_two))
    ):
        sent(skv, a2a_send.at[stage, 0])
        sent(sq, a2a_send.at[stage, 1])
        ring_sent(stage, kv)
        sent(so, back_send.at[stage])
    feats_copy.wait()
    result_copy.wait()


def per_device(q1, k1, v1, nbr, x2, w_view_out, norm_gain, w_qkv, w_out):
    anywhere = pl.BlockSpec(memory_space=pl.ANY)
    dma = pltpu.SemaphoreType.DMA
    stage_buffers = [
        pltpu.VMEM((ROWS, LANES), BF),
        pltpu.VMEM((ROWS, LANES), BF),
        pltpu.VMEM((ROWS, LANES), BF),
        pltpu.VMEM((VIEWS * ROWS, LANES), BF),
        pltpu.VMEM((ROWS, LANES), BF),
        pltpu.VMEM((ROWS, LANES), BF),
    ]
    return tuple(pl.pallas_call(
        kernel,
        out_shape=(
            jax.ShapeDtypeStruct((1, MY_ROWS, WIDTH), F32),
            jax.ShapeDtypeStruct((1, MY_ROWS, WIDTH), F32),
        ),
        in_specs=[pl.BlockSpec(memory_space=pltpu.SMEM)] + [anywhere] * 8,
        out_specs=(anywhere, anywhere),
        scratch_shapes=[pltpu.VMEM((MY_ROWS, WIDTH), BF)] * 4
        + [
            pltpu.VMEM((1, WIDTH), F32),
            pltpu.VMEM((WIDTH, WIDTH), BF),
            pltpu.VMEM((WIDTH, 3 * WIDTH), BF),
            pltpu.VMEM((WIDTH, WIDTH), BF),
        ]
        + stage_buffers * 2
        + [
            pltpu.VMEM((1, ROWS), F32),
            pltpu.VMEM((LANES, ROWS), F32),
            pltpu.VMEM((MY_ROWS, WIDTH), F32),
            pltpu.VMEM((MY_ROWS, WIDTH), F32),
            dma((5,)),
            dma((3,)),
            dma((2,)),
            dma((2, 2)),
            dma((2,)),
            dma((2, SUB)),
            dma((2, 2)),
            dma((2, 2, Z // 2 * SUB)),
            dma((2,)),
            dma((2, Z)),
            dma((2,)),
            dma((2,)),
        ],
        compiler_params=pltpu.CompilerParams(
            collective_id=0, has_side_effects=True, vmem_limit_bytes=56 * 1024 * 1024
        ),
    )(nbr, q1, k1, v1, x2, w_view_out, norm_gain.reshape(1, -1), w_qkv, w_out))


def solution(mesh):
    return jax.shard_map(
        per_device,
        mesh=mesh,
        in_specs=(
            P("view", "tok", None),
            P("view", "tok", None),
            P("view", "tok", None),
            P("view", None),
            P("view", "tok", None),
            P(),
            P(),
            P(),
            P(),
        ),
        out_specs=(P("view", "tok", None), P("view", "tok", None)),
        check_vma=False,
    )
```

```python
import math

import jax
import jax.numpy as jnp
from jax import lax
from jax.experimental import pallas as pl
from jax.experimental.pallas import tpu as pltpu
from jax.sharding import PartitionSpec as P

MESH = pl.DeviceIdType.MESH
BF = jnp.bfloat16
F32 = jnp.float32

EPSILON = 1e-06
NEGATIVE = -1e30
START_MAX = -3e38
HD = 64
LANES = 2 * HD
Z = 8
HEADS = 16
TOKS = 16
MY_ROWS = 32
HALF = MY_ROWS // 2
WIDTH = HEADS * HD
ROWS = TOKS * MY_ROWS
VIEWS = 2 * Z
SUB = 4
PIECE = ROWS // SUB
EXP2_SCALE = HD ** (-0.5) * math.log2(math.e)


def wait_bytes(like, sem):
    pltpu.make_async_copy(like, like, sem).wait()


def rows_of(ref, start, count):
    return ref.at[pl.ds(pl.multiple_of(start, count if count < 128 else 128), count), :]


def pack(q_of, k_of, v_of, sq, skv):
    low = lax.broadcasted_iota(jnp.int32, (MY_ROWS, LANES), 1) < HD
    low_half = lax.broadcasted_iota(jnp.int32, (HALF, LANES), 1) < HD
    for pair in range(HEADS // 2):
        q, k, v = q_of(pair), k_of(pair), v_of(pair)
        turned_q, turned_k, turned_v = (pltpu.roll(part, HD, 1) for part in (q, k, v))
        first, second = 2 * pair * MY_ROWS, (2 * pair + 1) * MY_ROWS
        sq[2 * pair * HALF : (2 * pair + 1) * HALF, :] = jnp.where(low_half, q[:HALF], turned_q[HALF:]).astype(BF)
        sq[(2 * pair + 1) * HALF : (2 * pair + 2) * HALF, :] = jnp.where(low_half, turned_q[:HALF], q[HALF:]).astype(BF)
        skv[first : first + MY_ROWS, :] = jnp.where(low, k, turned_v).astype(BF)
        skv[second : second + MY_ROWS, :] = jnp.where(low, turned_k, v).astype(BF)


def kernel(
    nbr, q1, k1, v1, x2, w_view_out, norm_gain, w_qkv, w_out,
    feats_out, lrm_out,
    q_in, k_in, v_in, x_in, gain_in, wv, wqkv, wo,
    sq_one, skv_one, rq_one, kv_one, so_one, ro_one,
    sq_two, skv_two, rq_two, kv_two, so_two, ro_two,
    mask_out, mask_in, qb, scores_a, scores_b, top_a, top_b, peak, acc, feats, result,
    load_sem, weight_sem, out_sem, a2a_send, a2a_q, a2a_kv, ring_send, ring_recv, pair_send, pair_recv, back_send, back_recv, mask_sem,
):
    view = lax.axis_index("view")
    tok = lax.axis_index("tok")
    z, y_hi = view // 2, view % 2
    core = tok % 2
    my_head = y_hi * 8 + tok // 8 * 4 + tok // 2 % 4
    my_view = z * 2 + core
    at_home = core == y_hi
    right = (z + 1) % Z * 2 + y_hi
    left = (z + Z - 1) % Z * 2 + y_hi
    partner = tok + 1 - 2 * core

    loads = [
        pltpu.make_async_copy(src, dst, load_sem.at[i])
        for i, (src, dst) in enumerate(
            ((q1.at[0], q_in), (k1.at[0], k_in), (v1.at[0], v_in), (x2.at[0], x_in), (norm_gain, gain_in))
        )
    ]
    weights = [
        pltpu.make_async_copy(src, dst, weight_sem.at[i])
        for i, (src, dst) in enumerate(((w_view_out, wv), (w_qkv, wqkv), (w_out, wo)))
    ]
    for copy in loads:
        copy.start()

    def head_device(head):
        return (z * 2 + head // 8, head // 4 % 2 * 8 + head % 4 * 2 + y_hi)

    def row_device(member):
        return (my_view, member)

    barrier = pltpu.get_barrier_semaphore()

    def greet(i, _):
        head_view, head_tok = head_device(i)

        @pl.when(jnp.logical_or(head_view != view, head_tok != tok))
        def _():
            pl.semaphore_signal(barrier, inc=1, device_id=(head_view, head_tok), device_id_type=MESH)

        @pl.when(jnp.logical_or(my_view != view, i != tok))
        def _():
            pl.semaphore_signal(barrier, inc=1, device_id=(my_view, i), device_id_type=MESH)

        return 0

    lax.fori_loop(0, TOKS, greet, 0)
    pl.semaphore_signal(barrier, inc=1, device_id=(right, tok), device_id_type=MESH)
    pl.semaphore_signal(barrier, inc=1, device_id=(left, tok), device_id_type=MESH)
    pl.semaphore_signal(barrier, inc=1, device_id=(view, partner), device_id_type=MESH)

    for copy in weights:
        copy.start()

    lane = lax.broadcasted_iota(jnp.int32, (1, LANES), 1)
    low_ones = jnp.where(lane < HD, 1.0, 0.0).astype(BF)
    high_ones = jnp.where(lane < HD, 0.0, 1.0).astype(BF)

    def all_to_all(stage, sq, skv, rq, kv):
        def send(src_of, dst, which, sem):
            def body(i, _):
                head = (my_head + i) % HEADS
                head_view, head_tok = head_device(head)
                mine = jnp.logical_and(head_view == view, head_tok == tok)

                @pl.when(mine)
                def _():
                    pltpu.make_async_copy(src_of(head), dst, sem).start()

                @pl.when(jnp.logical_not(mine))
                def _():
                    pltpu.make_async_remote_copy(
                        src_ref=src_of(head),
                        dst_ref=dst,
                        send_sem=a2a_send.at[stage, which],
                        recv_sem=sem,
                        device_id=(head_view, head_tok),
                        device_id_type=MESH,
                    ).start()

                return 0

            lax.fori_loop(0, HEADS, body, 0)

        send(
            lambda head: rows_of(skv, head * MY_ROWS, MY_ROWS),
            rows_of(kv, view * ROWS + tok * MY_ROWS, MY_ROWS),
            0,
            a2a_kv.at[stage, tok * MY_ROWS // PIECE],
        )
        send(
            lambda head: rows_of(sq, head * HALF, HALF), rows_of(rq, tok * HALF, HALF), 1, a2a_q.at[stage]
        )

    def sent(like, rows, sem):
        @pl.when(at_home)
        def _():
            wait_bytes(like.at[pl.ds(0, (HEADS - 1) * rows), :], sem)

        @pl.when(jnp.logical_not(at_home))
        def _():
            wait_bytes(like.at[pl.ds(0, HEADS * rows), :], sem)

    def ring_piece(stage, kv, direction, step, sub):
        from_z = (z + Z - step) % Z if direction == 0 else (z + step) % Z
        block = rows_of(kv, (from_z * 2 + core) * ROWS + sub * PIECE, PIECE)
        pltpu.make_async_remote_copy(
            src_ref=block,
            dst_ref=block,
            send_sem=ring_send.at[stage, direction],
            recv_sem=ring_recv.at[stage, direction, step * SUB + sub],
            device_id=(right if direction == 0 else left, tok),
            device_id_type=MESH,
        ).start()

    def to_partner(stage, kv, from_z, sub, slot):
        block = rows_of(kv, (from_z * 2 + core) * ROWS + sub * PIECE, PIECE)
        pltpu.make_async_remote_copy(
            src_ref=block,
            dst_ref=block,
            send_sem=pair_send.at[stage],
            recv_sem=pair_recv.at[stage, slot],
            device_id=(view, partner),
            device_id_type=MESH,
        ).start()

    halves = (slice(0, ROWS // 2), slice(ROWS // 2, ROWS))

    def block_of(kv, which):
        return kv[pl.ds(pl.multiple_of(which * ROWS, ROWS), ROWS), :]

    def score(kv, which, masked, scores, top):
        keys = block_of(kv, which)
        if masked:
            keys = keys * low_ones + jnp.where(lane == HD + which, 1.0, 0.0).astype(BF)
        for cols in halves:
            part = lax.dot_general(
                keys, qb[cols, :], (((1,), (1,)), ((), ())), preferred_element_type=F32
            )
            scores[:, cols] = part
            top[:, cols] = jnp.max(part, axis=0, keepdims=True)

    def weigh(kv, which, scores, top):
        values = block_of(kv, which) * high_ones + low_ones
        for cols in halves:
            old = peak[:, cols]
            new = jnp.maximum(old, top[:, cols])
            factor = jnp.exp2((old - new) * EXP2_SCALE)
            weights16 = jnp.exp2((scores[:, cols] - new) * EXP2_SCALE).astype(BF)
            part = lax.dot_general(
                values, weights16, (((0,), (0,)), ((), ())), preferred_element_type=F32
            )
            acc[:, cols] = acc[:, cols] * factor + part
            peak[:, cols] = new

    def attend(stage, rq, kv, masked):
        peak[...] = jnp.full_like(peak, START_MAX)
        acc[...] = jnp.zeros_like(acc)
        for sub in range(SUB):
            wait_bytes(rows_of(kv, my_view * ROWS + sub * PIECE, PIECE), a2a_kv.at[stage, sub])
            ring_piece(stage, kv, 0, 0, sub)
            ring_piece(stage, kv, 1, 0, sub)
            to_partner(stage, kv, z, sub, 0)
        wait_bytes(rq, a2a_q.at[stage])
        extra = mask_in[0:1, :].astype(F32) if masked else jnp.zeros((1, LANES), F32)
        both = rq[...].astype(F32)
        qb[halves[0], :] = jnp.where(lane < HD, both, extra).astype(BF)
        qb[halves[1], :] = jnp.where(lane < HD, pltpu.roll(both, HD, 1), extra).astype(BF)

        def piece_of(step, sub, direction):
            from_z = (z + Z - step) % Z if direction == 0 else (z + step) % Z
            slot = 2 * step - 1 + direction
            block = rows_of(kv, (from_z * 2 + core) * ROWS + sub * PIECE, PIECE)
            wait_bytes(block, ring_recv.at[stage, direction, (step - 1) * SUB + sub])
            if direction == 0:
                go_on = jnp.logical_or(step < Z // 2 - 1, sub < SUB // 2)
            else:
                go_on = jnp.logical_or(step < Z // 2 - 1, sub >= SUB // 2)

            @pl.when(jnp.logical_and(step < Z // 2, go_on))
            def _():
                ring_piece(stage, kv, direction, step, sub)

            to_partner(stage, kv, from_z, sub, jnp.minimum(slot, Z - 1))

        def pieces(step, sub):
            last = step == Z // 2

            @pl.when(jnp.logical_or(jnp.logical_not(last), sub < SUB // 2))
            def _():
                piece_of(step, sub, 0)

            @pl.when(jnp.logical_or(jnp.logical_not(last), sub >= SUB // 2))
            def _():
                piece_of(step, sub, 1)

        def view_of(chip_z, whose):
            return chip_z * 2 + core + whose * (1 - 2 * core)

        def from_partner(which, slot):
            wait_bytes(rows_of(kv, which * ROWS, ROWS), pair_recv.at[stage, slot])

        a, b = (scores_a, top_a), (scores_b, top_b)
        pieces(1, 0)
        score(kv, view_of(z, 0), masked, *a)
        pieces(1, 1)
        from_partner(view_of(z, 1), 0)
        score(kv, view_of(z, 1), masked, *b)
        weigh(kv, view_of(z, 0), *a)
        pieces(1, 2)
        pieces(1, 3)

        def two_blocks(i, before):
            behind, whose = i // 2 + 1, i % 2
            step = behind + 1
            right_view = view_of((z + Z - behind) % Z, whose)
            left_view = view_of((z + behind) % Z, whose)
            pieces(step, whose * 2)

            @pl.when(whose == 1)
            def _():
                from_partner(right_view, 2 * behind - 1)
                from_partner(left_view, 2 * behind)

            score(kv, right_view, masked, *a)
            weigh(kv, before, *b)
            pieces(step, whose * 2 + 1)
            score(kv, left_view, masked, *b)
            weigh(kv, right_view, *a)
            return left_view

        before = lax.fori_loop(0, Z - 2, two_blocks, view_of(z, 1))
        far = (z + Z // 2) % Z
        score(kv, view_of(far, 0), masked, *a)
        weigh(kv, before, *b)
        from_partner(view_of(far, 1), Z - 1)
        score(kv, view_of(far, 1), masked, *b)
        weigh(kv, view_of(far, 0), *a)
        weigh(kv, view_of(far, 1), *b)

    def ring_sent(stage, kv):
        for direction in range(2):
            wait_bytes(kv.at[pl.ds(0, ((Z // 2 - 1) * SUB + SUB // 2) * PIECE), :], ring_send.at[stage, direction])
        wait_bytes(kv.at[pl.ds(0, Z * ROWS), :], pair_send.at[stage])

    def send_back(stage, so, ro):
        first, second = (acc[HD:, cols] * (1.0 / acc[0:1, cols]) for cols in halves)
        so[...] = jnp.transpose(jnp.concatenate([first, second], axis=0)).astype(BF)

        def send(i, _):
            member = (tok + i) % TOKS
            mine = jnp.logical_and(my_view == view, member == tok)
            src = rows_of(so, member * HALF, HALF)
            dst = rows_of(ro, my_head * HALF, HALF)

            @pl.when(mine)
            def _():
                pltpu.make_async_copy(src, dst, back_recv.at[stage]).start()

            @pl.when(jnp.logical_not(mine))
            def _():
                pltpu.make_async_remote_copy(
                    src_ref=src,
                    dst_ref=dst,
                    send_sem=back_send.at[stage],
                    recv_sem=back_recv.at[stage],
                    device_id=(my_view, member),
                    device_id_type=MESH,
                ).start()

            return 0

        lax.fori_loop(0, TOKS, send, 0)
        wait_bytes(ro, back_recv.at[stage])

    def side_by_side(ro):
        low = lax.broadcasted_iota(jnp.int32, (HALF, LANES), 1) < HD
        parts = []
        for pair in range(HEADS // 2):
            first = ro[2 * pair * HALF : (2 * pair + 1) * HALF, :].astype(F32)
            second = ro[(2 * pair + 1) * HALF : (2 * pair + 2) * HALF, :].astype(F32)
            early = jnp.where(low, first, pltpu.roll(second, HD, 1))
            late = jnp.where(low, pltpu.roll(first, HD, 1), second)
            parts.append(jnp.concatenate([early, late], axis=0))
        return jnp.concatenate(parts, axis=1)

    def unit(values):
        return values * lax.rsqrt(jnp.mean(values * values, axis=-1, keepdims=True) + EPSILON)

    for copy in loads[:3]:
        copy.wait()
    lanes = lax.broadcasted_iota(jnp.int32, mask_out.shape, 1)
    wanted = lanes == HD + view
    for i in range(nbr.shape[1]):
        wanted = jnp.logical_or(wanted, lanes == HD + nbr[0, i])
    mask_out[...] = jnp.where(jnp.logical_or(wanted, lanes >= HD + VIEWS), 0.0, NEGATIVE).astype(BF)

    def cut(ref):
        return lambda pair: ref[:, pair * LANES : (pair + 1) * LANES].astype(F32)

    pack(cut(q_in), cut(k_in), cut(v_in), sq_one, skv_one)
    pl.semaphore_wait(barrier, jnp.where(at_home, 2 * TOKS + 1, 2 * TOKS + 3))
    all_to_all(0, sq_one, skv_one, rq_one, kv_one)

    @pl.when(at_home)
    def _():
        pltpu.make_async_copy(mask_out, mask_in, mask_sem.at[1]).start()

    @pl.when(jnp.logical_not(at_home))
    def _():
        pltpu.make_async_remote_copy(
            src_ref=mask_out,
            dst_ref=mask_in,
            send_sem=mask_sem.at[0],
            recv_sem=mask_sem.at[1],
            device_id=(my_view, tok - core + y_hi),
            device_id_type=MESH,
        ).start()
        wait_bytes(mask_out, mask_sem.at[0])

    wait_bytes(mask_in, mask_sem.at[1])
    attend(0, rq_one, kv_one, True)
    send_back(0, so_one, ro_one)

    attn = side_by_side(ro_one)
    feats_f32 = unit(attn)
    feats[...] = feats_f32
    feats_copy = pltpu.make_async_copy(feats, feats_out.at[0], out_sem.at[0])
    feats_copy.start()
    for copy in loads[3:]:
        copy.wait()
    weights[0].wait()
    hidden = x_in[...].astype(F32) + jnp.dot(feats_f32.astype(BF), wv[...], preferred_element_type=F32)
    normed = (unit(hidden) * gain_in[...]).astype(BF)
    weights[1].wait()
    projected = [
        jnp.dot(normed, wqkv[:, part * WIDTH : (part + 1) * WIDTH], preferred_element_type=F32)
        for part in range(3)
    ]

    def cut_value(value):
        return lambda pair: value[:, pair * LANES : (pair + 1) * LANES]

    pack(*(cut_value(part) for part in projected), sq_two, skv_two)

    all_to_all(1, sq_two, skv_two, rq_two, kv_two)
    attend(1, rq_two, kv_two, False)
    send_back(1, so_two, ro_two)
    unit_rows = unit(side_by_side(ro_two)).astype(BF)
    weights[2].wait()
    result[...] = jnp.dot(unit_rows, wo[...], preferred_element_type=F32)
    result_copy = pltpu.make_async_copy(result, lrm_out.at[0], out_sem.at[1])
    result_copy.start()

    for stage, (sq, skv, kv, so) in enumerate(
        ((sq_one, skv_one, kv_one, so_one), (sq_two, skv_two, kv_two, so_two))
    ):
        sent(skv, MY_ROWS, a2a_send.at[stage, 0])
        sent(sq, HALF, a2a_send.at[stage, 1])
        ring_sent(stage, kv)
        sent(so, HALF, back_send.at[stage])
    feats_copy.wait()
    result_copy.wait()


def per_device(q1, k1, v1, nbr, x2, w_view_out, norm_gain, w_qkv, w_out):
    anywhere = pl.BlockSpec(memory_space=pl.ANY)
    dma = pltpu.SemaphoreType.DMA
    stage_buffers = [
        pltpu.VMEM((HEADS * HALF, LANES), BF),
        pltpu.VMEM((HEADS * MY_ROWS, LANES), BF),
        pltpu.VMEM((TOKS * HALF, LANES), BF),
        pltpu.VMEM((VIEWS * ROWS, LANES), BF),
        pltpu.VMEM((TOKS * HALF, LANES), BF),
        pltpu.VMEM((HEADS * HALF, LANES), BF),
    ]
    return tuple(pl.pallas_call(
        kernel,
        out_shape=(
            jax.ShapeDtypeStruct((1, MY_ROWS, WIDTH), F32),
            jax.ShapeDtypeStruct((1, MY_ROWS, WIDTH), F32),
        ),
        in_specs=[pl.BlockSpec(memory_space=pltpu.SMEM)] + [anywhere] * 8,
        out_specs=(anywhere, anywhere),
        scratch_shapes=[pltpu.VMEM((MY_ROWS, WIDTH), BF)] * 4
        + [
            pltpu.VMEM((1, WIDTH), F32),
            pltpu.VMEM((WIDTH, WIDTH), BF),
            pltpu.VMEM((WIDTH, 3 * WIDTH), BF),
            pltpu.VMEM((WIDTH, WIDTH), BF),
        ]
        + stage_buffers * 2
        + [
            pltpu.VMEM((HALF, LANES), BF),
            pltpu.VMEM((HALF, LANES), BF),
            pltpu.VMEM((ROWS, LANES), BF),
            pltpu.VMEM((ROWS, ROWS), F32),
            pltpu.VMEM((ROWS, ROWS), F32),
            pltpu.VMEM((1, ROWS), F32),
            pltpu.VMEM((1, ROWS), F32),
            pltpu.VMEM((1, ROWS), F32),
            pltpu.VMEM((LANES, ROWS), F32),
            pltpu.VMEM((MY_ROWS, WIDTH), F32),
            pltpu.VMEM((MY_ROWS, WIDTH), F32),
            dma((5,)),
            dma((3,)),
            dma((2,)),
            dma((2, 2)),
            dma((2,)),
            dma((2, SUB)),
            dma((2, 2)),
            dma((2, 2, Z // 2 * SUB)),
            dma((2,)),
            dma((2, Z)),
            dma((2,)),
            dma((2,)),
            dma((2,)),
        ],
        compiler_params=pltpu.CompilerParams(
            collective_id=0, has_side_effects=True, vmem_limit_bytes=56 * 1024 * 1024
        ),
    )(nbr, q1, k1, v1, x2, w_view_out, norm_gain.reshape(1, -1), w_qkv, w_out))


def solution(mesh):
    return jax.shard_map(
        per_device,
        mesh=mesh,
        in_specs=(
            P("view", "tok", None),
            P("view", "tok", None),
            P("view", "tok", None),
            P("view", None),
            P("view", "tok", None),
            P(),
            P(),
            P(),
            P(),
        ),
        out_specs=(P("view", "tok", None), P("view", "tok", None)),
        check_vma=False,
    )
```

```python
import math

import jax
import jax.numpy as jnp
from jax import lax
from jax.experimental import pallas as pl
from jax.experimental.pallas import tpu as pltpu
from jax.sharding import PartitionSpec as P

MESH = pl.DeviceIdType.MESH
BF = jnp.bfloat16
F32 = jnp.float32

EPSILON = 1e-06
NEGATIVE = -1e30
START_MAX = -3e38
HD = 64
LANES = 2 * HD
Z = 8
HEADS = 16
TOKS = 16
MY_ROWS = 32
HALF = MY_ROWS // 2
WIDTH = HEADS * HD
ROWS = TOKS * MY_ROWS
VIEWS = 2 * Z
SUB = 4
PIECE = ROWS // SUB
EXP2_SCALE = HD ** (-0.5) * math.log2(math.e)


def wait_bytes(like, sem):
    pltpu.make_async_copy(like, like, sem).wait()


def rows_of(ref, start, count):
    return ref.at[pl.ds(pl.multiple_of(start, count if count < 128 else 128), count), :]


def pack_keys(k_of, v_of, skv):
    low = lax.broadcasted_iota(jnp.int32, (MY_ROWS, LANES), 1) < HD
    for pair in range(HEADS // 2):
        k, v = k_of(pair), v_of(pair)
        first, second = 2 * pair * MY_ROWS, (2 * pair + 1) * MY_ROWS
        skv[first : first + MY_ROWS, :] = jnp.where(low, k, pltpu.roll(v, HD, 1)).astype(BF)
        skv[second : second + MY_ROWS, :] = jnp.where(low, pltpu.roll(k, HD, 1), v).astype(BF)


def pack_queries(q_of, sq):
    low = lax.broadcasted_iota(jnp.int32, (HALF, LANES), 1) < HD
    for pair in range(HEADS // 2):
        q = q_of(pair)
        turned = pltpu.roll(q, HD, 1)
        sq[2 * pair * HALF : (2 * pair + 1) * HALF, :] = jnp.where(low, q[:HALF], turned[HALF:]).astype(BF)
        sq[(2 * pair + 1) * HALF : (2 * pair + 2) * HALF, :] = jnp.where(low, turned[:HALF], q[HALF:]).astype(BF)


def kernel(
    nbr_hbm, q1, k1, v1, x2, w_view_out, norm_gain, w_qkv, w_out,
    feats_out, lrm_out,
    nbr, q_in, k_in, v_in, x_in, gain_in, wv, wqkv, wo,
    sq_one, skv_one, rq_one, kv_one, so_one, ro_one,
    sq_two, skv_two, rq_two, kv_two, so_two, ro_two,
    mask_out, mask_in, qb, scores_a, scores_b, top_a, top_b, peak, acc, feats, result,
    load_sem, weight_sem, out_sem, a2a_send, a2a_q, a2a_kv, ring_send, ring_recv, pair_send, pair_recv, back_send, back_recv, mask_sem,
):
    view = lax.axis_index("view")
    tok = lax.axis_index("tok")
    z, y_hi = view // 2, view % 2
    core = tok % 2
    my_head = y_hi * 8 + tok // 8 * 4 + tok // 2 % 4
    my_view = z * 2 + core
    at_home = core == y_hi
    right = (z + 1) % Z * 2 + y_hi
    left = (z + Z - 1) % Z * 2 + y_hi
    partner = tok + 1 - 2 * core

    loads = [
        pltpu.make_async_copy(src, dst, load_sem.at[i])
        for i, (src, dst) in enumerate(
            ((k1.at[0], k_in), (v1.at[0], v_in), (q1.at[0], q_in), (nbr_hbm, nbr), (x2.at[0], x_in), (norm_gain, gain_in))
        )
    ]
    weights = [
        pltpu.make_async_copy(src, dst, weight_sem.at[i])
        for i, (src, dst) in enumerate(((w_view_out, wv), (w_qkv, wqkv), (w_out, wo)))
    ]
    for copy in loads:
        copy.start()

    def head_device(head):
        return (z * 2 + head // 8, head // 4 % 2 * 8 + head % 4 * 2 + y_hi)

    def row_device(member):
        return (my_view, member)

    barrier = pltpu.get_barrier_semaphore()

    def greet(i, _):
        head_view, head_tok = head_device(i)

        @pl.when(jnp.logical_or(head_view != view, head_tok != tok))
        def _():
            pl.semaphore_signal(barrier, inc=1, device_id=(head_view, head_tok), device_id_type=MESH)

        @pl.when(jnp.logical_or(my_view != view, i != tok))
        def _():
            pl.semaphore_signal(barrier, inc=1, device_id=(my_view, i), device_id_type=MESH)

        return 0

    lax.fori_loop(0, TOKS, greet, 0)
    pl.semaphore_signal(barrier, inc=1, device_id=(right, tok), device_id_type=MESH)
    pl.semaphore_signal(barrier, inc=1, device_id=(left, tok), device_id_type=MESH)
    pl.semaphore_signal(barrier, inc=1, device_id=(view, partner), device_id_type=MESH)

    for copy in weights:
        copy.start()

    lane = lax.broadcasted_iota(jnp.int32, (1, LANES), 1)
    low_ones = jnp.where(lane < HD, 1.0, 0.0).astype(BF)
    high_ones = jnp.where(lane < HD, 0.0, 1.0).astype(BF)

    def spread(src_of, dst, device_of, send_sem, recv_sem):
        def remote(i):
            pltpu.make_async_remote_copy(
                src_ref=src_of(i),
                dst_ref=dst,
                send_sem=send_sem,
                recv_sem=recv_sem,
                device_id=device_of(i),
                device_id_type=MESH,
            ).start()

        def body(i, _):
            remote(i)
            return 0

        lax.fori_loop(1, TOKS, body, 0)

        @pl.when(at_home)
        def _():
            pltpu.make_async_copy(src_of(0), dst, recv_sem).start()

        @pl.when(jnp.logical_not(at_home))
        def _():
            remote(0)

    def nth_head(i):
        return (my_head + i) % HEADS

    def send_keys(stage, skv, kv):
        spread(
            lambda i: rows_of(skv, nth_head(i) * MY_ROWS, MY_ROWS),
            rows_of(kv, view * ROWS + tok * MY_ROWS, MY_ROWS),
            lambda i: head_device(nth_head(i)),
            a2a_send.at[stage, 0],
            a2a_kv.at[stage, tok * MY_ROWS // PIECE],
        )

    def send_queries(stage, sq, rq):
        spread(
            lambda i: rows_of(sq, nth_head(i) * HALF, HALF),
            rows_of(rq, tok * HALF, HALF),
            lambda i: head_device(nth_head(i)),
            a2a_send.at[stage, 1],
            a2a_q.at[stage],
        )

    def sent(like, rows, sem):
        @pl.when(at_home)
        def _():
            wait_bytes(like.at[pl.ds(0, (HEADS - 1) * rows), :], sem)

        @pl.when(jnp.logical_not(at_home))
        def _():
            wait_bytes(like.at[pl.ds(0, HEADS * rows), :], sem)

    def ring_piece(stage, kv, direction, step, sub):
        from_z = (z + Z - step) % Z if direction == 0 else (z + step) % Z
        block = rows_of(kv, (from_z * 2 + core) * ROWS + sub * PIECE, PIECE)
        pltpu.make_async_remote_copy(
            src_ref=block,
            dst_ref=block,
            send_sem=ring_send.at[stage, direction],
            recv_sem=ring_recv.at[stage, direction, step * SUB + sub],
            device_id=(right if direction == 0 else left, tok),
            device_id_type=MESH,
        ).start()

    def to_partner(stage, kv, from_z, sub, slot):
        block = rows_of(kv, (from_z * 2 + core) * ROWS + sub * PIECE, PIECE)
        pltpu.make_async_remote_copy(
            src_ref=block,
            dst_ref=block,
            send_sem=pair_send.at[stage],
            recv_sem=pair_recv.at[stage, slot],
            device_id=(view, partner),
            device_id_type=MESH,
        ).start()

    halves = (slice(0, ROWS // 2), slice(ROWS // 2, ROWS))

    def block_of(kv, which):
        return kv[pl.ds(pl.multiple_of(which * ROWS, ROWS), ROWS), :]

    def score(kv, which, masked, scores, top):
        keys = block_of(kv, which)
        if masked:
            keys = keys * low_ones + jnp.where(lane == HD + which, 1.0, 0.0).astype(BF)
        for cols in halves:
            part = lax.dot_general(
                keys, qb[cols, :], (((1,), (1,)), ((), ())), preferred_element_type=F32
            )
            scores[:, cols] = part
            top[:, cols] = jnp.max(part, axis=0, keepdims=True)

    def weigh(kv, which, scores, top):
        values = block_of(kv, which) * high_ones + low_ones
        for cols in halves:
            old = peak[:, cols]
            new = jnp.maximum(old, top[:, cols])
            factor = jnp.exp2((old - new) * EXP2_SCALE)
            weights16 = jnp.exp2((scores[:, cols] - new) * EXP2_SCALE).astype(BF)
            part = lax.dot_general(
                values, weights16, (((0,), (0,)), ((), ())), preferred_element_type=F32
            )
            acc[:, cols] = acc[:, cols] * factor + part
            peak[:, cols] = new

    def attend(stage, rq, kv, masked):
        peak[...] = jnp.full_like(peak, START_MAX)
        acc[...] = jnp.zeros_like(acc)
        for sub in range(SUB):
            wait_bytes(rows_of(kv, my_view * ROWS + sub * PIECE, PIECE), a2a_kv.at[stage, sub])
            ring_piece(stage, kv, 0, 0, sub)
            ring_piece(stage, kv, 1, 0, sub)
        for sub in range(SUB):
            to_partner(stage, kv, z, sub, 0)
        wait_bytes(rq, a2a_q.at[stage])
        if masked:
            wait_bytes(mask_in, mask_sem.at[1])
        extra = mask_in[0:1, :].astype(F32) if masked else jnp.zeros((1, LANES), F32)
        both = rq[...].astype(F32)
        qb[halves[0], :] = jnp.where(lane < HD, both, extra).astype(BF)
        qb[halves[1], :] = jnp.where(lane < HD, pltpu.roll(both, HD, 1), extra).astype(BF)

        def piece_of(step, sub, direction):
            from_z = (z + Z - step) % Z if direction == 0 else (z + step) % Z
            block = rows_of(kv, (from_z * 2 + core) * ROWS + sub * PIECE, PIECE)
            wait_bytes(block, ring_recv.at[stage, direction, (step - 1) * SUB + sub])
            return from_z

        def pieces(step, sub):
            right_z = piece_of(step, sub, 0)

            @pl.when(jnp.logical_or(step < Z // 2 - 1, sub < SUB // 2))
            def _():
                ring_piece(stage, kv, 0, step, sub)

            left_z = piece_of(step, sub, 1)

            @pl.when(jnp.logical_or(step < Z // 2 - 1, sub >= SUB // 2))
            def _():
                ring_piece(stage, kv, 1, step, sub)

            to_partner(stage, kv, right_z, sub, 2 * step - 1)
            to_partner(stage, kv, left_z, sub, 2 * step)

        def last_pieces(sub):
            for direction, piece in ((0, sub), (1, SUB // 2 + sub)):
                to_partner(stage, kv, piece_of(Z // 2, piece, direction), piece, Z - 1)

        def view_of(chip_z, whose):
            return chip_z * 2 + core + whose * (1 - 2 * core)

        def from_partner(which, slot):
            wait_bytes(rows_of(kv, which * ROWS, ROWS), pair_recv.at[stage, slot])

        a, b = (scores_a, top_a), (scores_b, top_b)
        pieces(1, 0)
        score(kv, view_of(z, 0), masked, *a)
        pieces(1, 1)
        from_partner(view_of(z, 1), 0)
        score(kv, view_of(z, 1), masked, *b)
        weigh(kv, view_of(z, 0), *a)
        pieces(1, 2)
        pieces(1, 3)

        def two_blocks(behind, whose, before, ahead):
            right_view = view_of((z + Z - behind) % Z, whose)
            left_view = view_of((z + behind) % Z, whose)
            ahead(0)

            @pl.when(whose == 1)
            def _():
                from_partner(right_view, 2 * behind - 1)
                from_partner(left_view, 2 * behind)

            score(kv, right_view, masked, *a)
            weigh(kv, before, *b)
            ahead(1)
            score(kv, left_view, masked, *b)
            weigh(kv, right_view, *a)
            return left_view

        def middle(i, before):
            behind, whose = i // 2 + 1, i % 2
            return two_blocks(behind, whose, before, lambda j: pieces(behind + 1, whose * 2 + j))

        before = lax.fori_loop(0, Z - 4, middle, view_of(z, 1))
        far = (z + Z // 2) % Z

        def final(whose, before):
            return two_blocks(Z // 2 - 1, whose, before, lambda j: None)

        before = lax.fori_loop(0, 2, final, before)
        weigh(kv, before, *b)
        last_pieces(0)
        last_pieces(1)
        score(kv, view_of(far, 0), masked, *a)
        weigh(kv, view_of(far, 0), *a)
        from_partner(view_of(far, 1), Z - 1)
        score(kv, view_of(far, 1), masked, *b)
        weigh(kv, view_of(far, 1), *b)

    def ring_sent(stage, kv):
        for direction in range(2):
            wait_bytes(kv.at[pl.ds(0, ((Z // 2 - 1) * SUB + SUB // 2) * PIECE), :], ring_send.at[stage, direction])
        wait_bytes(kv.at[pl.ds(0, Z * ROWS), :], pair_send.at[stage])

    def send_back(stage, so, ro):
        first, second = (acc[HD:, cols] * (1.0 / acc[0:1, cols]) for cols in halves)
        so[...] = jnp.transpose(jnp.concatenate([first, second], axis=0)).astype(BF)

        spread(
            lambda i: rows_of(so, (tok + i) % TOKS * HALF, HALF),
            rows_of(ro, my_head * HALF, HALF),
            lambda i: (my_view, (tok + i) % TOKS),
            back_send.at[stage],
            back_recv.at[stage],
        )
        wait_bytes(ro, back_recv.at[stage])

    def side_by_side(ro):
        low = lax.broadcasted_iota(jnp.int32, (HALF, LANES), 1) < HD
        parts = []
        for pair in range(HEADS // 2):
            first = ro[2 * pair * HALF : (2 * pair + 1) * HALF, :].astype(F32)
            second = ro[(2 * pair + 1) * HALF : (2 * pair + 2) * HALF, :].astype(F32)
            early = jnp.where(low, first, pltpu.roll(second, HD, 1))
            late = jnp.where(low, pltpu.roll(first, HD, 1), second)
            parts.append(jnp.concatenate([early, late], axis=0))
        return jnp.concatenate(parts, axis=1)

    def unit(values):
        return values * lax.rsqrt(jnp.mean(values * values, axis=-1, keepdims=True) + EPSILON)

    for copy in loads[:2]:
        copy.wait()

    def cut(ref):
        return lambda pair: ref[:, pair * LANES : (pair + 1) * LANES].astype(F32)

    pack_keys(cut(k_in), cut(v_in), skv_one)
    pl.semaphore_wait(barrier, jnp.where(at_home, 2 * TOKS + 1, 2 * TOKS + 3))
    send_keys(0, skv_one, kv_one)
    for copy in loads[2:4]:
        copy.wait()
    pack_queries(cut(q_in), sq_one)
    send_queries(0, sq_one, rq_one)
    lanes = lax.broadcasted_iota(jnp.int32, mask_out.shape, 1)
    wanted = lanes == HD + view
    for i in range(nbr.shape[1]):
        wanted = jnp.logical_or(wanted, lanes == HD + nbr[0, i])
    mask_out[...] = jnp.where(jnp.logical_or(wanted, lanes >= HD + VIEWS), 0.0, NEGATIVE).astype(BF)

    @pl.when(at_home)
    def _():
        pltpu.make_async_copy(mask_out, mask_in, mask_sem.at[1]).start()

    @pl.when(jnp.logical_not(at_home))
    def _():
        pltpu.make_async_remote_copy(
            src_ref=mask_out,
            dst_ref=mask_in,
            send_sem=mask_sem.at[0],
            recv_sem=mask_sem.at[1],
            device_id=(my_view, tok - core + y_hi),
            device_id_type=MESH,
        ).start()

    attend(0, rq_one, kv_one, True)
    send_back(0, so_one, ro_one)

    attn = side_by_side(ro_one)
    feats_f32 = unit(attn)
    feats_out[0] = feats_f32
    for copy in loads[4:]:
        copy.wait()
    weights[0].wait()
    hidden = x_in[...].astype(F32) + jnp.dot(feats_f32.astype(BF), wv[...], preferred_element_type=F32)
    normed = (unit(hidden) * gain_in[...]).astype(BF)
    weights[1].wait()

    def project(part):
        return jnp.dot(normed, wqkv[:, part * WIDTH : (part + 1) * WIDTH], preferred_element_type=F32)

    def cut_value(value):
        return lambda pair: value[:, pair * LANES : (pair + 1) * LANES]

    pack_keys(cut_value(project(1)), cut_value(project(2)), skv_two)
    send_keys(1, skv_two, kv_two)
    pack_queries(cut_value(project(0)), sq_two)
    send_queries(1, sq_two, rq_two)

    attend(1, rq_two, kv_two, False)
    send_back(1, so_two, ro_two)
    unit_rows = unit(side_by_side(ro_two)).astype(BF)
    weights[2].wait()
    lrm_out[0] = jnp.dot(unit_rows, wo[...], preferred_element_type=F32)

    for stage, (sq, skv, kv, so) in enumerate(
        ((sq_one, skv_one, kv_one, so_one), (sq_two, skv_two, kv_two, so_two))
    ):
        sent(skv, MY_ROWS, a2a_send.at[stage, 0])
        sent(sq, HALF, a2a_send.at[stage, 1])
        ring_sent(stage, kv)
        sent(so, HALF, back_send.at[stage])

    @pl.when(jnp.logical_not(at_home))
    def _():
        wait_bytes(mask_out, mask_sem.at[0])


def per_device(q1, k1, v1, nbr, x2, w_view_out, norm_gain, w_qkv, w_out):
    anywhere = pl.BlockSpec(memory_space=pl.ANY)
    dma = pltpu.SemaphoreType.DMA
    stage_buffers = [
        pltpu.VMEM((HEADS * HALF, LANES), BF),
        pltpu.VMEM((HEADS * MY_ROWS, LANES), BF),
        pltpu.VMEM((TOKS * HALF, LANES), BF),
        pltpu.VMEM((VIEWS * ROWS, LANES), BF),
        pltpu.VMEM((TOKS * HALF, LANES), BF),
        pltpu.VMEM((HEADS * HALF, LANES), BF),
    ]
    return tuple(pl.pallas_call(
        kernel,
        out_shape=(
            pltpu.VMEM((1, MY_ROWS, WIDTH), F32),
            pltpu.VMEM((1, MY_ROWS, WIDTH), F32),
        ),
        in_specs=[anywhere] * 9,
        out_specs=(pl.BlockSpec(memory_space=pltpu.VMEM),) * 2,
        scratch_shapes=[pltpu.SMEM((1, 7), jnp.int32)]
        + [pltpu.VMEM((MY_ROWS, WIDTH), BF)] * 4
        + [
            pltpu.VMEM((1, WIDTH), F32),
            pltpu.VMEM((WIDTH, WIDTH), BF),
            pltpu.VMEM((WIDTH, 3 * WIDTH), BF),
            pltpu.VMEM((WIDTH, WIDTH), BF),
        ]
        + stage_buffers * 2
        + [
            pltpu.VMEM((HALF, LANES), BF),
            pltpu.VMEM((HALF, LANES), BF),
            pltpu.VMEM((ROWS, LANES), BF),
            pltpu.VMEM((ROWS, ROWS), F32),
            pltpu.VMEM((ROWS, ROWS), F32),
            pltpu.VMEM((1, ROWS), F32),
            pltpu.VMEM((1, ROWS), F32),
            pltpu.VMEM((1, ROWS), F32),
            pltpu.VMEM((LANES, ROWS), F32),
            pltpu.VMEM((MY_ROWS, WIDTH), F32),
            pltpu.VMEM((MY_ROWS, WIDTH), F32),
            dma((6,)),
            dma((3,)),
            dma((2,)),
            dma((2, 2)),
            dma((2,)),
            dma((2, SUB)),
            dma((2, 2)),
            dma((2, 2, Z // 2 * SUB)),
            dma((2,)),
            dma((2, Z)),
            dma((2,)),
            dma((2,)),
            dma((2,)),
        ],
        compiler_params=pltpu.CompilerParams(
            collective_id=0, has_side_effects=True, vmem_limit_bytes=56 * 1024 * 1024
        ),
    )(nbr, q1, k1, v1, x2, w_view_out, norm_gain.reshape(1, -1), w_qkv, w_out))


def solution(mesh):
    return jax.shard_map(
        per_device,
        mesh=mesh,
        in_specs=(
            P("view", "tok", None),
            P("view", "tok", None),
            P("view", "tok", None),
            P("view", None),
            P("view", "tok", None),
            P(),
            P(),
            P(),
            P(),
        ),
        out_specs=(P("view", "tok", None), P("view", "tok", None)),
        check_vma=False,
    )
```

```python
import math

import jax
import jax.numpy as jnp
from jax import lax
from jax.experimental import pallas as pl
from jax.experimental.pallas import tpu as pltpu
from jax.sharding import PartitionSpec as P

MESH = pl.DeviceIdType.MESH
BF = jnp.bfloat16
F32 = jnp.float32

EPSILON = 1e-06
NEGATIVE = -1e30
START_MAX = -3e38
HD = 64
LANES = 2 * HD
Z = 8
HEADS = 16
TOKS = 16
MY_ROWS = 32
HALF = MY_ROWS // 2
WIDTH = HEADS * HD
ROWS = TOKS * MY_ROWS
VIEWS = 2 * Z
SUB = 4
PIECE = ROWS // SUB
EXP2_SCALE = HD ** (-0.5) * math.log2(math.e)


def ring_distance(offset):
    return min(offset % 4, -offset % 4)


CHIP_ORDER = sorted(
    ((dx, dy) for dy in range(4) for dx in range(4)), key=lambda at: -ring_distance(at[0]) - ring_distance(at[1])
)
MEMBER_ORDER = sorted(
    ((dx, dy, dc) for dy in range(2) for dx in range(4) for dc in range(2)),
    key=lambda at: (-ring_distance(at[0]), -at[1], -at[2]),
)


def wait_bytes(like, sem):
    pltpu.make_async_copy(like, like, sem).wait()


def rows_of(ref, start, count):
    return ref.at[pl.ds(pl.multiple_of(start, count if count < 128 else 128), count), :]


def pack_keys(k_of, v_of, skv):
    low = lax.broadcasted_iota(jnp.int32, (MY_ROWS, LANES), 1) < HD
    for pair in range(HEADS // 2):
        k, v = k_of(pair), v_of(pair)
        first, second = 2 * pair * MY_ROWS, (2 * pair + 1) * MY_ROWS
        skv[first : first + MY_ROWS, :] = jnp.where(low, k, pltpu.roll(v, HD, 1)).astype(BF)
        skv[second : second + MY_ROWS, :] = jnp.where(low, pltpu.roll(k, HD, 1), v).astype(BF)


def pack_queries(q_of, sq):
    low = lax.broadcasted_iota(jnp.int32, (HALF, LANES), 1) < HD
    for pair in range(HEADS // 2):
        q = q_of(pair)
        turned = pltpu.roll(q, HD, 1)
        sq[2 * pair * HALF : (2 * pair + 1) * HALF, :] = jnp.where(low, q[:HALF], turned[HALF:]).astype(BF)
        sq[(2 * pair + 1) * HALF : (2 * pair + 2) * HALF, :] = jnp.where(low, turned[:HALF], q[HALF:]).astype(BF)


def kernel(
    nbr_hbm, q1, k1, v1, x2, w_view_out, norm_gain, w_qkv, w_out,
    feats_out, lrm_out,
    nbr, q_in, k_in, v_in, x_in, gain_in, wv, wqkv, wo,
    sqs, skvs, rqs, kvs, sos, ros,
    normed, mask_out, mask_in, qb, scores_a, scores_b, top_a, top_b, peak, acc,
    load_sem, weight_sem, a2a_send, a2a_q, a2a_kv, ring_send, ring_recv, pair_send, pair_recv, back_send, back_recv, mask_sem,
):
    view = lax.axis_index("view")
    tok = lax.axis_index("tok")
    z, y_hi = view // 2, view % 2
    core = tok % 2
    x, y_lo = tok // 2 % 4, tok // 8
    y = y_hi * 2 + y_lo
    my_head = y * 4 + x
    my_view = z * 2 + core
    at_home = core == y_hi
    right = (z + 1) % Z * 2 + y_hi
    left = (z + Z - 1) % Z * 2 + y_hi
    partner = tok + 1 - 2 * core

    loads = [
        pltpu.make_async_copy(src, dst, load_sem.at[i])
        for i, (src, dst) in enumerate(
            ((k1.at[0], k_in), (v1.at[0], v_in), (q1.at[0], q_in), (nbr_hbm, nbr), (x2.at[0], x_in), (norm_gain, gain_in))
        )
    ]
    weights = [
        pltpu.make_async_copy(src, dst, weight_sem.at[i])
        for i, (src, dst) in enumerate(((w_view_out, wv), (w_qkv, wqkv), (w_out, wo)))
    ]
    for copy in loads:
        copy.start()

    def head_device(head):
        return (z * 2 + head // 8, head // 4 % 2 * 8 + head % 4 * 2 + y_hi)

    def row_device(member):
        return (my_view, member)

    barrier = pltpu.get_barrier_semaphore()

    def greet(i, _):
        head_view, head_tok = head_device(i)

        @pl.when(jnp.logical_or(head_view != view, head_tok != tok))
        def _():
            pl.semaphore_signal(barrier, inc=1, device_id=(head_view, head_tok), device_id_type=MESH)

        @pl.when(jnp.logical_or(my_view != view, i != tok))
        def _():
            pl.semaphore_signal(barrier, inc=1, device_id=(my_view, i), device_id_type=MESH)

        return 0

    lax.fori_loop(0, TOKS, greet, 0)
    pl.semaphore_signal(barrier, inc=1, device_id=(right, tok), device_id_type=MESH)
    pl.semaphore_signal(barrier, inc=1, device_id=(left, tok), device_id_type=MESH)
    pl.semaphore_signal(barrier, inc=1, device_id=(view, partner), device_id_type=MESH)

    for copy in weights:
        copy.start()

    lane = lax.broadcasted_iota(jnp.int32, (1, LANES), 1)
    low_ones = jnp.where(lane < HD, 1.0, 0.0).astype(BF)
    high_ones = jnp.where(lane < HD, 0.0, 1.0).astype(BF)

    def spread(src_of, dst, device_of, send_sem, recv_sem):
        def remote(i):
            pltpu.make_async_remote_copy(
                src_ref=src_of(i),
                dst_ref=dst,
                send_sem=send_sem,
                recv_sem=recv_sem,
                device_id=device_of(i),
                device_id_type=MESH,
            ).start()

        for i in range(TOKS - 1):
            remote(i)

        @pl.when(at_home)
        def _():
            pltpu.make_async_copy(src_of(TOKS - 1), dst, recv_sem).start()

        @pl.when(jnp.logical_not(at_home))
        def _():
            remote(TOKS - 1)

    def nth_head(i):
        dx, dy = CHIP_ORDER[i]
        return (y + dy) % 4 * 4 + (x + dx) % 4

    def nth_member(i):
        dx, dy, dc = MEMBER_ORDER[i]
        return (y_lo + dy) % 2 * 8 + (x + dx) % 4 * 2 + (core + dc) % 2

    def send_keys(stage, skv, kv):
        spread(
            lambda i: rows_of(skv, nth_head(i) * MY_ROWS, MY_ROWS),
            rows_of(kv, view * ROWS + tok * MY_ROWS, MY_ROWS),
            lambda i: head_device(nth_head(i)),
            a2a_send.at[stage, 0],
            a2a_kv.at[stage, tok * MY_ROWS // PIECE],
        )

    def send_queries(stage, sq, rq):
        spread(
            lambda i: rows_of(sq, nth_head(i) * HALF, HALF),
            rows_of(rq, tok * HALF, HALF),
            lambda i: head_device(nth_head(i)),
            a2a_send.at[stage, 1],
            a2a_q.at[stage],
        )

    def sent(like, rows, sem):
        @pl.when(at_home)
        def _():
            wait_bytes(like.at[pl.ds(0, (HEADS - 1) * rows), :], sem)

        @pl.when(jnp.logical_not(at_home))
        def _():
            wait_bytes(like.at[pl.ds(0, HEADS * rows), :], sem)

    def ring_piece(stage, kv, direction, step, sub):
        from_z = (z + Z - step) % Z if direction == 0 else (z + step) % Z
        block = rows_of(kv, (from_z * 2 + core) * ROWS + sub * PIECE, PIECE)
        pltpu.make_async_remote_copy(
            src_ref=block,
            dst_ref=block,
            send_sem=ring_send.at[stage, direction],
            recv_sem=ring_recv.at[stage, direction, step * SUB + sub],
            device_id=(right if direction == 0 else left, tok),
            device_id_type=MESH,
        ).start()

    def to_partner(stage, kv, from_z, sub, slot):
        block = rows_of(kv, (from_z * 2 + core) * ROWS + sub * PIECE, PIECE)
        pltpu.make_async_remote_copy(
            src_ref=block,
            dst_ref=block,
            send_sem=pair_send.at[stage],
            recv_sem=pair_recv.at[stage, slot],
            device_id=(view, partner),
            device_id_type=MESH,
        ).start()

    halves = (slice(0, ROWS // 2), slice(ROWS // 2, ROWS))

    def block_of(kv, which):
        return kv[pl.ds(pl.multiple_of(which * ROWS, ROWS), ROWS), :]

    def score(kv, which, scores, top):
        keys = block_of(kv, which) * low_ones + jnp.where(lane == HD + which, 1.0, 0.0).astype(BF)
        for cols in halves:
            part = lax.dot_general(
                keys, qb[cols, :], (((1,), (1,)), ((), ())), preferred_element_type=F32
            )
            scores[:, cols] = part
            top[:, cols] = jnp.max(part, axis=0, keepdims=True)

    def weigh(kv, which, scores, top):
        values = block_of(kv, which) * high_ones + low_ones
        for cols in halves:
            old = peak[:, cols]
            new = jnp.maximum(old, top[:, cols])
            factor = jnp.exp2((old - new) * EXP2_SCALE)
            weights16 = jnp.exp2((scores[:, cols] - new) * EXP2_SCALE).astype(BF)
            part = lax.dot_general(
                values, weights16, (((0,), (0,)), ((), ())), preferred_element_type=F32
            )
            acc[:, cols] = acc[:, cols] * factor + part
            peak[:, cols] = new

    def attend(stage, rq, kv):
        peak[...] = jnp.full_like(peak, START_MAX)
        acc[...] = jnp.zeros_like(acc)
        for sub in range(SUB):
            wait_bytes(rows_of(kv, my_view * ROWS + sub * PIECE, PIECE), a2a_kv.at[stage, sub])
            ring_piece(stage, kv, 0, 0, sub)
            ring_piece(stage, kv, 1, 0, sub)
        for sub in range(SUB):
            to_partner(stage, kv, z, sub, 0)
        wait_bytes(rq, a2a_q.at[stage])

        @pl.when(stage == 0)
        def _():
            wait_bytes(mask_in, mask_sem.at[1])

        extra = jnp.where(stage == 0, mask_in[0:1, :].astype(F32), 0.0)
        both = rq[...].astype(F32)
        qb[halves[0], :] = jnp.where(lane < HD, both, extra).astype(BF)
        qb[halves[1], :] = jnp.where(lane < HD, pltpu.roll(both, HD, 1), extra).astype(BF)

        def piece_of(step, sub, direction):
            from_z = (z + Z - step) % Z if direction == 0 else (z + step) % Z
            block = rows_of(kv, (from_z * 2 + core) * ROWS + sub * PIECE, PIECE)
            wait_bytes(block, ring_recv.at[stage, direction, (step - 1) * SUB + sub])
            return from_z

        def pieces(step, sub):
            right_z = piece_of(step, sub, 0)

            @pl.when(jnp.logical_or(step < Z // 2 - 1, sub < SUB // 2))
            def _():
                ring_piece(stage, kv, 0, step, sub)

            left_z = piece_of(step, sub, 1)

            @pl.when(jnp.logical_or(step < Z // 2 - 1, sub >= SUB // 2))
            def _():
                ring_piece(stage, kv, 1, step, sub)

            to_partner(stage, kv, right_z, sub, 2 * step - 1)
            to_partner(stage, kv, left_z, sub, 2 * step)

        def last_pieces(sub):
            for direction, piece in ((0, sub), (1, SUB // 2 + sub)):
                to_partner(stage, kv, piece_of(Z // 2, piece, direction), piece, Z - 1)

        def view_of(chip_z, whose):
            return chip_z * 2 + core + whose * (1 - 2 * core)

        def from_partner(which, slot):
            wait_bytes(rows_of(kv, which * ROWS, ROWS), pair_recv.at[stage, slot])

        a, b = (scores_a, top_a), (scores_b, top_b)
        pieces(1, 0)
        score(kv, view_of(z, 0), *a)
        pieces(1, 1)
        from_partner(view_of(z, 1), 0)
        score(kv, view_of(z, 1), *b)
        weigh(kv, view_of(z, 0), *a)
        pieces(1, 2)
        pieces(1, 3)

        def two_blocks(behind, whose, before, ahead):
            right_view = view_of((z + Z - behind) % Z, whose)
            left_view = view_of((z + behind) % Z, whose)
            ahead(0)

            @pl.when(whose == 1)
            def _():
                from_partner(right_view, 2 * behind - 1)
                from_partner(left_view, 2 * behind)

            score(kv, right_view, *a)
            weigh(kv, before, *b)
            ahead(1)
            score(kv, left_view, *b)
            weigh(kv, right_view, *a)
            return left_view

        def middle(i, before):
            behind, whose = i // 2 + 1, i % 2
            return two_blocks(behind, whose, before, lambda j: pieces(behind + 1, whose * 2 + j))

        before = lax.fori_loop(0, Z - 4, middle, view_of(z, 1))
        far = (z + Z // 2) % Z

        def final(whose, before):
            return two_blocks(Z // 2 - 1, whose, before, lambda j: None)

        before = lax.fori_loop(0, 2, final, before)
        weigh(kv, before, *b)
        last_pieces(0)
        last_pieces(1)
        score(kv, view_of(far, 0), *a)
        weigh(kv, view_of(far, 0), *a)
        from_partner(view_of(far, 1), Z - 1)
        score(kv, view_of(far, 1), *b)
        weigh(kv, view_of(far, 1), *b)

    def ring_sent(stage, kv):
        for direction in range(2):
            wait_bytes(kv.at[pl.ds(0, ((Z // 2 - 1) * SUB + SUB // 2) * PIECE), :], ring_send.at[stage, direction])
        wait_bytes(kv.at[pl.ds(0, Z * ROWS), :], pair_send.at[stage])

    def send_back(stage, so, ro):
        first, second = (acc[HD:, cols] * (1.0 / acc[0:1, cols]) for cols in halves)
        so[...] = jnp.transpose(jnp.concatenate([first, second], axis=0)).astype(BF)

        spread(
            lambda i: rows_of(so, nth_member(i) * HALF, HALF),
            rows_of(ro, my_head * HALF, HALF),
            lambda i: (my_view, nth_member(i)),
            back_send.at[stage],
            back_recv.at[stage],
        )
        wait_bytes(ro, back_recv.at[stage])

    def side_by_side(ro):
        low = lax.broadcasted_iota(jnp.int32, (HALF, LANES), 1) < HD
        parts = []
        for pair in range(HEADS // 2):
            first = ro[2 * pair * HALF : (2 * pair + 1) * HALF, :].astype(F32)
            second = ro[(2 * pair + 1) * HALF : (2 * pair + 2) * HALF, :].astype(F32)
            early = jnp.where(low, first, pltpu.roll(second, HD, 1))
            late = jnp.where(low, pltpu.roll(first, HD, 1), second)
            parts.append(jnp.concatenate([early, late], axis=0))
        return jnp.concatenate(parts, axis=1)

    def unit(values):
        return values * lax.rsqrt(jnp.mean(values * values, axis=-1, keepdims=True) + EPSILON)

    def cut(ref):
        return lambda pair: ref[:, pair * LANES : (pair + 1) * LANES].astype(F32)

    def cut_value(value):
        return lambda pair: value[:, pair * LANES : (pair + 1) * LANES]

    def project(part):
        return jnp.dot(
            normed[...], wqkv[:, part * WIDTH : (part + 1) * WIDTH], preferred_element_type=F32
        )

    for copy in loads[:2]:
        copy.wait()
    pack_keys(cut(k_in), cut(v_in), skvs.at[0])
    pl.semaphore_wait(barrier, jnp.where(at_home, 2 * TOKS + 1, 2 * TOKS + 3))

    def attention(stage, _):
        sq, skv, rq, kv, so, ro = (ref.at[stage] for ref in (sqs, skvs, rqs, kvs, sos, ros))
        send_keys(stage, skv, kv)

        @pl.when(stage == 0)
        def _():
            for copy in loads[2:4]:
                copy.wait()
            pack_queries(cut(q_in), sq)
            lanes = lax.broadcasted_iota(jnp.int32, mask_out.shape, 1)
            wanted = lanes == HD + view
            for i in range(nbr.shape[1]):
                wanted = jnp.logical_or(wanted, lanes == HD + nbr[0, i])
            mask_out[...] = jnp.where(jnp.logical_or(wanted, lanes >= HD + VIEWS), 0.0, NEGATIVE).astype(BF)

            @pl.when(at_home)
            def _():
                pltpu.make_async_copy(mask_out, mask_in, mask_sem.at[1]).start()

            @pl.when(jnp.logical_not(at_home))
            def _():
                pltpu.make_async_remote_copy(
                    src_ref=mask_out,
                    dst_ref=mask_in,
                    send_sem=mask_sem.at[0],
                    recv_sem=mask_sem.at[1],
                    device_id=(my_view, tok - core + y_hi),
                    device_id_type=MESH,
                ).start()

        @pl.when(stage == 1)
        def _():
            pack_queries(cut_value(project(0)), sq)

        send_queries(stage, sq, rq)
        attend(stage, rq, kv)
        send_back(stage, so, ro)
        rows = unit(side_by_side(ro))

        @pl.when(stage == 0)
        def _():
            feats_out[0] = rows
            for copy in loads[4:]:
                copy.wait()
            weights[0].wait()
            hidden = x_in[...].astype(F32) + jnp.dot(rows.astype(BF), wv[...], preferred_element_type=F32)
            normed[...] = (unit(hidden) * gain_in[...]).astype(BF)
            weights[1].wait()
            pack_keys(cut_value(project(1)), cut_value(project(2)), skvs.at[1])

        @pl.when(stage == 1)
        def _():
            weights[2].wait()
            lrm_out[0] = jnp.dot(rows.astype(BF), wo[...], preferred_element_type=F32)

        return 0

    lax.fori_loop(0, 2, attention, 0)

    def finish(stage, _):
        sent(skvs.at[stage], MY_ROWS, a2a_send.at[stage, 0])
        sent(sqs.at[stage], HALF, a2a_send.at[stage, 1])
        ring_sent(stage, kvs.at[stage])
        sent(sos.at[stage], HALF, back_send.at[stage])
        return 0

    lax.fori_loop(0, 2, finish, 0)

    @pl.when(jnp.logical_not(at_home))
    def _():
        wait_bytes(mask_out, mask_sem.at[0])


def per_device(q1, k1, v1, nbr, x2, w_view_out, norm_gain, w_qkv, w_out):
    anywhere = pl.BlockSpec(memory_space=pl.ANY)
    dma = pltpu.SemaphoreType.DMA
    stage_buffers = [
        pltpu.VMEM((2, HEADS * HALF, LANES), BF),
        pltpu.VMEM((2, HEADS * MY_ROWS, LANES), BF),
        pltpu.VMEM((2, TOKS * HALF, LANES), BF),
        pltpu.VMEM((2, VIEWS * ROWS, LANES), BF),
        pltpu.VMEM((2, TOKS * HALF, LANES), BF),
        pltpu.VMEM((2, HEADS * HALF, LANES), BF),
        pltpu.VMEM((MY_ROWS, WIDTH), BF),
    ]
    return tuple(pl.pallas_call(
        kernel,
        out_shape=(
            pltpu.VMEM((1, MY_ROWS, WIDTH), F32),
            pltpu.VMEM((1, MY_ROWS, WIDTH), F32),
        ),
        in_specs=[anywhere] * 9,
        out_specs=(pl.BlockSpec(memory_space=pltpu.VMEM),) * 2,
        scratch_shapes=[pltpu.SMEM((1, 7), jnp.int32)]
        + [pltpu.VMEM((MY_ROWS, WIDTH), BF)] * 4
        + [
            pltpu.VMEM((1, WIDTH), F32),
            pltpu.VMEM((WIDTH, WIDTH), BF),
            pltpu.VMEM((WIDTH, 3 * WIDTH), BF),
            pltpu.VMEM((WIDTH, WIDTH), BF),
        ]
        + stage_buffers
        + [
            pltpu.VMEM((HALF, LANES), BF),
            pltpu.VMEM((HALF, LANES), BF),
            pltpu.VMEM((ROWS, LANES), BF),
            pltpu.VMEM((ROWS, ROWS), F32),
            pltpu.VMEM((ROWS, ROWS), F32),
            pltpu.VMEM((1, ROWS), F32),
            pltpu.VMEM((1, ROWS), F32),
            pltpu.VMEM((1, ROWS), F32),
            pltpu.VMEM((LANES, ROWS), F32),
            dma((6,)),
            dma((3,)),
            dma((2, 2)),
            dma((2,)),
            dma((2, SUB)),
            dma((2, 2)),
            dma((2, 2, Z // 2 * SUB)),
            dma((2,)),
            dma((2, Z)),
            dma((2,)),
            dma((2,)),
            dma((2,)),
        ],
        compiler_params=pltpu.CompilerParams(
            collective_id=0, has_side_effects=True, vmem_limit_bytes=56 * 1024 * 1024
        ),
    )(nbr, q1, k1, v1, x2, w_view_out, norm_gain.reshape(1, -1), w_qkv, w_out))


def solution(mesh):
    return jax.shard_map(
        per_device,
        mesh=mesh,
        in_specs=(
            P("view", "tok", None),
            P("view", "tok", None),
            P("view", "tok", None),
            P("view", None),
            P("view", "tok", None),
            P(),
            P(),
            P(),
            P(),
        ),
        out_specs=(P("view", "tok", None), P("view", "tok", None)),
        check_vma=False,
    )
```

```python
import math

import jax
import jax.numpy as jnp
from jax import lax
from jax.experimental import pallas as pl
from jax.experimental.pallas import tpu as pltpu
from jax.sharding import PartitionSpec as P

MESH = pl.DeviceIdType.MESH
BF = jnp.bfloat16
F32 = jnp.float32

EPSILON = 1e-06
NEGATIVE = -1e30
START_MAX = -3e38
HD = 64
LANES = 2 * HD
Z = 8
HEADS = 16
TOKS = 16
MY_ROWS = 32
HALF = MY_ROWS // 2
WIDTH = HEADS * HD
ROWS = TOKS * MY_ROWS
VIEWS = 2 * Z
SUB = 4
PIECE = ROWS // SUB
TWICE = 1
EXP2_SCALE = HD ** (-0.5) * math.log2(math.e)


def ring_distance(offset):
    return min(offset % 4, -offset % 4)


CHIP_ORDER = sorted(
    ((dx, dy) for dy in range(4) for dx in range(4)), key=lambda at: -ring_distance(at[0]) - ring_distance(at[1])
)
MEMBER_ORDER = sorted(
    ((dx, dy, dc) for dy in range(2) for dx in range(4) for dc in range(2)),
    key=lambda at: (-ring_distance(at[0]), -at[1], -at[2]),
)


def wait_bytes(like, sem):
    pltpu.make_async_copy(like, like, sem).wait()


def rows_of(ref, start, count):
    return ref.at[pl.ds(pl.multiple_of(start, count if count < 128 else 128), count), :]


def pack_keys(k_of, v_of, skv):
    low = lax.broadcasted_iota(jnp.int32, (MY_ROWS, LANES), 1) < HD
    for pair in range(HEADS // 2):
        k, v = k_of(pair), v_of(pair)
        first, second = 2 * pair * MY_ROWS, (2 * pair + 1) * MY_ROWS
        skv[first : first + MY_ROWS, :] = jnp.where(low, k, pltpu.roll(v, HD, 1)).astype(BF)
        skv[second : second + MY_ROWS, :] = jnp.where(low, pltpu.roll(k, HD, 1), v).astype(BF)


def pack_queries(q_of, sq):
    low = lax.broadcasted_iota(jnp.int32, (HALF, LANES), 1) < HD
    for pair in range(HEADS // 2):
        q = q_of(pair)
        turned = pltpu.roll(q, HD, 1)
        sq[2 * pair * HALF : (2 * pair + 1) * HALF, :] = jnp.where(low, q[:HALF], turned[HALF:]).astype(BF)
        sq[(2 * pair + 1) * HALF : (2 * pair + 2) * HALF, :] = jnp.where(low, turned[:HALF], q[HALF:]).astype(BF)


def kernel(
    nbr_hbm, q1, k1, v1, x2, w_view_out, norm_gain, w_qkv, w_out,
    feats_out, lrm_out,
    nbr, q_in, k_in, v_in, x_in, gain_in, wv, wqkv, wo,
    sqs, skvs, rqs, kvs, sos, ros,
    normed, mask_out, mask_in, qb, scores_a, scores_b, top_a, top_b, peak, acc,
    load_sem, weight_sem, a2a_send, a2a_q, a2a_kv, ring_send, ring_recv, pair_send, pair_recv, back_send, back_recv, mask_sem,
):
    view = lax.axis_index("view")
    tok = lax.axis_index("tok")
    z, y_hi = view // 2, view % 2
    core = tok % 2
    x, y_lo = tok // 2 % 4, tok // 8
    y = y_hi * 2 + y_lo
    my_head = y * 4 + x
    my_view = z * 2 + core
    at_home = core == y_hi
    right = (z + 1) % Z * 2 + y_hi
    left = (z + Z - 1) % Z * 2 + y_hi
    partner = tok + 1 - 2 * core

    loads = [
        pltpu.make_async_copy(src, dst, load_sem.at[i])
        for i, (src, dst) in enumerate(
            ((k1.at[0], k_in), (v1.at[0], v_in), (q1.at[0], q_in), (nbr_hbm, nbr), (x2.at[0], x_in), (norm_gain, gain_in))
        )
    ]
    weights = [
        pltpu.make_async_copy(src, dst, weight_sem.at[i])
        for i, (src, dst) in enumerate(((w_view_out, wv), (w_qkv, wqkv), (w_out, wo)))
    ]
    for copy in loads:
        copy.start()

    def head_device(head):
        return (z * 2 + head // 8, head // 4 % 2 * 8 + head % 4 * 2 + y_hi)

    def row_device(member):
        return (my_view, member)

    barrier = pltpu.get_barrier_semaphore()

    def greet(i, _):
        head_view, head_tok = head_device(i)

        @pl.when(jnp.logical_or(head_view != view, head_tok != tok))
        def _():
            pl.semaphore_signal(barrier, inc=1, device_id=(head_view, head_tok), device_id_type=MESH)

        @pl.when(jnp.logical_or(my_view != view, i != tok))
        def _():
            pl.semaphore_signal(barrier, inc=1, device_id=(my_view, i), device_id_type=MESH)

        return 0

    lax.fori_loop(0, TOKS, greet, 0)
    pl.semaphore_signal(barrier, inc=1, device_id=(right, tok), device_id_type=MESH)
    pl.semaphore_signal(barrier, inc=1, device_id=(left, tok), device_id_type=MESH)
    pl.semaphore_signal(barrier, inc=1, device_id=(view, partner), device_id_type=MESH)
    pl.semaphore_signal(barrier, inc=1, device_id=(right, partner), device_id_type=MESH)
    pl.semaphore_signal(barrier, inc=1, device_id=(left, partner), device_id_type=MESH)

    for copy in weights:
        copy.start()

    lane = lax.broadcasted_iota(jnp.int32, (1, LANES), 1)
    low_ones = jnp.where(lane < HD, 1.0, 0.0).astype(BF)
    high_ones = jnp.where(lane < HD, 0.0, 1.0).astype(BF)

    def spread(src_of, dst, device_of, send_sem, recv_sem):
        def remote(i):
            pltpu.make_async_remote_copy(
                src_ref=src_of(i),
                dst_ref=dst,
                send_sem=send_sem,
                recv_sem=recv_sem,
                device_id=device_of(i),
                device_id_type=MESH,
            ).start()

        for i in range(TOKS - 1):
            remote(i)

        @pl.when(at_home)
        def _():
            pltpu.make_async_copy(src_of(TOKS - 1), dst, recv_sem).start()

        @pl.when(jnp.logical_not(at_home))
        def _():
            remote(TOKS - 1)

    def nth_head(i):
        dx, dy = CHIP_ORDER[i]
        return (y + dy) % 4 * 4 + (x + dx) % 4

    def nth_member(i):
        dx, dy, dc = MEMBER_ORDER[i]
        return (y_lo + dy) % 2 * 8 + (x + dx) % 4 * 2 + (core + dc) % 2

    def send_keys(stage, skv, kv):
        spread(
            lambda i: rows_of(skv, nth_head(i) * MY_ROWS, MY_ROWS),
            rows_of(kv, view * ROWS + tok * MY_ROWS, MY_ROWS),
            lambda i: head_device(nth_head(i)),
            a2a_send.at[stage, 0],
            a2a_kv.at[stage, tok * MY_ROWS // PIECE],
        )

    def send_queries(stage, sq, rq):
        spread(
            lambda i: rows_of(sq, nth_head(i) * HALF, HALF),
            rows_of(rq, tok * HALF, HALF),
            lambda i: head_device(nth_head(i)),
            a2a_send.at[stage, 1],
            a2a_q.at[stage],
        )

    def sent(like, rows, sem):
        @pl.when(at_home)
        def _():
            wait_bytes(like.at[pl.ds(0, (HEADS - 1) * rows), :], sem)

        @pl.when(jnp.logical_not(at_home))
        def _():
            wait_bytes(like.at[pl.ds(0, HEADS * rows), :], sem)

    def ring_piece(stage, kv, direction, step, sub):
        from_z = (z + Z - step) % Z if direction == 0 else (z + step) % Z
        block = rows_of(kv, (from_z * 2 + core) * ROWS + sub * PIECE, PIECE)
        pltpu.make_async_remote_copy(
            src_ref=block,
            dst_ref=block,
            send_sem=ring_send.at[stage, direction],
            recv_sem=ring_recv.at[stage, direction, step * SUB + sub],
            device_id=(right if direction == 0 else left, tok),
            device_id_type=MESH,
        ).start()

    def to_partner(stage, kv, from_z, sub, slot, chip=None):
        block = rows_of(kv, (from_z * 2 + core) * ROWS + sub * PIECE, PIECE)
        pltpu.make_async_remote_copy(
            src_ref=block,
            dst_ref=block,
            send_sem=pair_send.at[stage],
            recv_sem=pair_recv.at[stage, slot],
            device_id=(view if chip is None else chip, partner),
            device_id_type=MESH,
        ).start()

    halves = (slice(0, ROWS // 2), slice(ROWS // 2, ROWS))

    def block_of(kv, which):
        return kv[pl.ds(pl.multiple_of(which * ROWS, ROWS), ROWS), :]

    def score(kv, which, scores, top):
        keys = block_of(kv, which) * low_ones + jnp.where(lane == HD + which, 1.0, 0.0).astype(BF)
        for cols in halves:
            part = lax.dot_general(
                keys, qb[cols, :], (((1,), (1,)), ((), ())), preferred_element_type=F32
            )
            scores[:, cols] = part
            top[:, cols] = jnp.max(part, axis=0, keepdims=True)

    def weigh(kv, which, scores, top):
        values = block_of(kv, which) * high_ones + low_ones
        for cols in halves:
            old = peak[:, cols]
            new = jnp.maximum(old, top[:, cols])
            factor = jnp.exp2((old - new) * EXP2_SCALE)
            weights16 = jnp.exp2((scores[:, cols] - new) * EXP2_SCALE).astype(BF)
            part = lax.dot_general(
                values, weights16, (((0,), (0,)), ((), ())), preferred_element_type=F32
            )
            acc[:, cols] = acc[:, cols] * factor + part
            peak[:, cols] = new

    def attend(stage, rq, kv):
        peak[...] = jnp.full_like(peak, START_MAX)
        acc[...] = jnp.zeros_like(acc)
        for sub in range(SUB):
            wait_bytes(rows_of(kv, my_view * ROWS + sub * PIECE, PIECE), a2a_kv.at[stage, sub])
            ring_piece(stage, kv, 0, 0, sub)
            ring_piece(stage, kv, 1, 0, sub)
        for sub in range(SUB):
            to_partner(stage, kv, z, sub, 0)
        wait_bytes(rq, a2a_q.at[stage])

        @pl.when(stage == 0)
        def _():
            wait_bytes(mask_in, mask_sem.at[1])

        extra = jnp.where(stage == 0, mask_in[0:1, :].astype(F32), 0.0)
        both = rq[...].astype(F32)
        qb[halves[0], :] = jnp.where(lane < HD, both, extra).astype(BF)
        qb[halves[1], :] = jnp.where(lane < HD, pltpu.roll(both, HD, 1), extra).astype(BF)

        def piece_of(step, sub, direction):
            from_z = (z + Z - step) % Z if direction == 0 else (z + step) % Z
            block = rows_of(kv, (from_z * 2 + core) * ROWS + sub * PIECE, PIECE)
            wait_bytes(block, ring_recv.at[stage, direction, (step - 1) * SUB + sub])
            return from_z

        def pieces(step, sub):
            right_z = piece_of(step, sub, 0)

            @pl.when(jnp.logical_or(step < Z // 2 - 1, sub < SUB // 2))
            def _():
                ring_piece(stage, kv, 0, step, sub)

            left_z = piece_of(step, sub, 1)

            @pl.when(jnp.logical_or(step < Z // 2 - 1, sub >= SUB // 2))
            def _():
                ring_piece(stage, kv, 1, step, sub)

            for direction, from_z, chip in ((0, right_z, right), (1, left_z, left)):
                end = SUB // 2 * (direction + 1)

                @pl.when(jnp.logical_and(step == Z // 2 - 1, jnp.logical_and(sub >= end - TWICE, sub < end)))
                def _():
                    to_partner(stage, kv, from_z, sub, Z - 1, chip)

            to_partner(stage, kv, right_z, sub, 2 * step - 1)
            to_partner(stage, kv, left_z, sub, 2 * step)

        def last_pieces(sub):
            for direction, piece in ((0, sub), (1, SUB // 2 + sub)):
                from_z = piece_of(Z // 2, piece, direction)
                if sub < SUB // 2 - TWICE:
                    to_partner(stage, kv, from_z, piece, Z - 1)

        def view_of(chip_z, whose):
            return chip_z * 2 + core + whose * (1 - 2 * core)

        def from_partner(which, slot):
            wait_bytes(rows_of(kv, which * ROWS, ROWS), pair_recv.at[stage, slot])

        a, b = (scores_a, top_a), (scores_b, top_b)
        pieces(1, 0)
        score(kv, view_of(z, 0), *a)
        pieces(1, 1)
        from_partner(view_of(z, 1), 0)
        score(kv, view_of(z, 1), *b)
        weigh(kv, view_of(z, 0), *a)
        pieces(1, 2)
        pieces(1, 3)

        def two_blocks(behind, whose, before, ahead):
            right_view = view_of((z + Z - behind) % Z, whose)
            left_view = view_of((z + behind) % Z, whose)
            ahead(0)

            @pl.when(whose == 1)
            def _():
                from_partner(right_view, 2 * behind - 1)
                from_partner(left_view, 2 * behind)

            score(kv, right_view, *a)
            weigh(kv, before, *b)
            ahead(1)
            score(kv, left_view, *b)
            weigh(kv, right_view, *a)
            return left_view

        def middle(i, before):
            behind, whose = i // 2 + 1, i % 2
            return two_blocks(behind, whose, before, lambda j: pieces(behind + 1, whose * 2 + j))

        before = lax.fori_loop(0, Z - 4, middle, view_of(z, 1))
        far = (z + Z // 2) % Z

        def final(whose, before):
            return two_blocks(Z // 2 - 1, whose, before, lambda j: None)

        before = lax.fori_loop(0, 2, final, before)
        weigh(kv, before, *b)
        last_pieces(0)
        last_pieces(1)
        score(kv, view_of(far, 0), *a)
        from_partner(view_of(far, 1), Z - 1)
        score(kv, view_of(far, 1), *b)
        weigh(kv, view_of(far, 0), *a)
        weigh(kv, view_of(far, 1), *b)

    def ring_sent(stage, kv):
        for direction in range(2):
            wait_bytes(kv.at[pl.ds(0, ((Z // 2 - 1) * SUB + SUB // 2) * PIECE), :], ring_send.at[stage, direction])
        wait_bytes(kv.at[pl.ds(0, Z * ROWS), :], pair_send.at[stage])

    def send_back(stage, so, ro):
        first, second = (acc[HD:, cols] * (1.0 / acc[0:1, cols]) for cols in halves)
        so[...] = jnp.transpose(jnp.concatenate([first, second], axis=0)).astype(BF)

        spread(
            lambda i: rows_of(so, nth_member(i) * HALF, HALF),
            rows_of(ro, my_head * HALF, HALF),
            lambda i: (my_view, nth_member(i)),
            back_send.at[stage],
            back_recv.at[stage],
        )
        wait_bytes(ro, back_recv.at[stage])

    def side_by_side(ro):
        low = lax.broadcasted_iota(jnp.int32, (HALF, LANES), 1) < HD
        parts = []
        for pair in range(HEADS // 2):
            first = ro[2 * pair * HALF : (2 * pair + 1) * HALF, :].astype(F32)
            second = ro[(2 * pair + 1) * HALF : (2 * pair + 2) * HALF, :].astype(F32)
            early = jnp.where(low, first, pltpu.roll(second, HD, 1))
            late = jnp.where(low, pltpu.roll(first, HD, 1), second)
            parts.append(jnp.concatenate([early, late], axis=0))
        return jnp.concatenate(parts, axis=1)

    def unit(values):
        return values * lax.rsqrt(jnp.mean(values * values, axis=-1, keepdims=True) + EPSILON)

    def cut(ref):
        return lambda pair: ref[:, pair * LANES : (pair + 1) * LANES].astype(F32)

    def cut_value(value):
        return lambda pair: value[:, pair * LANES : (pair + 1) * LANES]

    def project(part):
        return jnp.dot(
            normed[...], wqkv[:, part * WIDTH : (part + 1) * WIDTH], preferred_element_type=F32
        )

    for copy in loads[:2]:
        copy.wait()
    pack_keys(cut(k_in), cut(v_in), skvs.at[0])
    pl.semaphore_wait(barrier, jnp.where(at_home, 2 * TOKS + 3, 2 * TOKS + 5))

    def attention(stage, _):
        sq, skv, rq, kv, so, ro = (ref.at[stage] for ref in (sqs, skvs, rqs, kvs, sos, ros))
        send_keys(stage, skv, kv)

        @pl.when(stage == 0)
        def _():
            for copy in loads[2:4]:
                copy.wait()
            pack_queries(cut(q_in), sq)
            lanes = lax.broadcasted_iota(jnp.int32, mask_out.shape, 1)
            wanted = lanes == HD + view
            for i in range(nbr.shape[1]):
                wanted = jnp.logical_or(wanted, lanes == HD + nbr[0, i])
            mask_out[...] = jnp.where(jnp.logical_or(wanted, lanes >= HD + VIEWS), 0.0, NEGATIVE).astype(BF)

            @pl.when(at_home)
            def _():
                pltpu.make_async_copy(mask_out, mask_in, mask_sem.at[1]).start()

            @pl.when(jnp.logical_not(at_home))
            def _():
                pltpu.make_async_remote_copy(
                    src_ref=mask_out,
                    dst_ref=mask_in,
                    send_sem=mask_sem.at[0],
                    recv_sem=mask_sem.at[1],
                    device_id=(my_view, tok - core + y_hi),
                    device_id_type=MESH,
                ).start()

        @pl.when(stage == 1)
        def _():
            pack_queries(cut_value(project(0)), sq)

        send_queries(stage, sq, rq)
        attend(stage, rq, kv)
        send_back(stage, so, ro)
        rows = unit(side_by_side(ro))

        @pl.when(stage == 0)
        def _():
            feats_out[0] = rows
            for copy in loads[4:]:
                copy.wait()
            weights[0].wait()
            hidden = x_in[...].astype(F32) + jnp.dot(rows.astype(BF), wv[...], preferred_element_type=F32)
            normed[...] = (unit(hidden) * gain_in[...]).astype(BF)
            weights[1].wait()
            pack_keys(cut_value(project(1)), cut_value(project(2)), skvs.at[1])

        @pl.when(stage == 1)
        def _():
            weights[2].wait()
            lrm_out[0] = jnp.dot(rows.astype(BF), wo[...], preferred_element_type=F32)

        return 0

    lax.fori_loop(0, 2, attention, 0)

    def finish(stage, _):
        sent(skvs.at[stage], MY_ROWS, a2a_send.at[stage, 0])
        sent(sqs.at[stage], HALF, a2a_send.at[stage, 1])
        ring_sent(stage, kvs.at[stage])
        sent(sos.at[stage], HALF, back_send.at[stage])
        return 0

    lax.fori_loop(0, 2, finish, 0)

    @pl.when(jnp.logical_not(at_home))
    def _():
        wait_bytes(mask_out, mask_sem.at[0])


def per_device(q1, k1, v1, nbr, x2, w_view_out, norm_gain, w_qkv, w_out):
    anywhere = pl.BlockSpec(memory_space=pl.ANY)
    dma = pltpu.SemaphoreType.DMA
    stage_buffers = [
        pltpu.VMEM((2, HEADS * HALF, LANES), BF),
        pltpu.VMEM((2, HEADS * MY_ROWS, LANES), BF),
        pltpu.VMEM((2, TOKS * HALF, LANES), BF),
        pltpu.VMEM((2, VIEWS * ROWS, LANES), BF),
        pltpu.VMEM((2, TOKS * HALF, LANES), BF),
        pltpu.VMEM((2, HEADS * HALF, LANES), BF),
        pltpu.VMEM((MY_ROWS, WIDTH), BF),
    ]
    return tuple(pl.pallas_call(
        kernel,
        out_shape=(
            pltpu.VMEM((1, MY_ROWS, WIDTH), F32),
            pltpu.VMEM((1, MY_ROWS, WIDTH), F32),
        ),
        in_specs=[anywhere] * 9,
        out_specs=(pl.BlockSpec(memory_space=pltpu.VMEM),) * 2,
        scratch_shapes=[pltpu.SMEM((1, 7), jnp.int32)]
        + [pltpu.VMEM((MY_ROWS, WIDTH), BF)] * 4
        + [
            pltpu.VMEM((1, WIDTH), F32),
            pltpu.VMEM((WIDTH, WIDTH), BF),
            pltpu.VMEM((WIDTH, 3 * WIDTH), BF),
            pltpu.VMEM((WIDTH, WIDTH), BF),
        ]
        + stage_buffers
        + [
            pltpu.VMEM((HALF, LANES), BF),
            pltpu.VMEM((HALF, LANES), BF),
            pltpu.VMEM((ROWS, LANES), BF),
            pltpu.VMEM((ROWS, ROWS), F32),
            pltpu.VMEM((ROWS, ROWS), F32),
            pltpu.VMEM((1, ROWS), F32),
            pltpu.VMEM((1, ROWS), F32),
            pltpu.VMEM((1, ROWS), F32),
            pltpu.VMEM((LANES, ROWS), F32),
            dma((6,)),
            dma((3,)),
            dma((2, 2)),
            dma((2,)),
            dma((2, SUB)),
            dma((2, 2)),
            dma((2, 2, Z // 2 * SUB)),
            dma((2,)),
            dma((2, Z)),
            dma((2,)),
            dma((2,)),
            dma((2,)),
        ],
        compiler_params=pltpu.CompilerParams(
            collective_id=0, has_side_effects=True, vmem_limit_bytes=56 * 1024 * 1024
        ),
    )(nbr, q1, k1, v1, x2, w_view_out, norm_gain.reshape(1, -1), w_qkv, w_out))


def solution(mesh):
    return jax.shard_map(
        per_device,
        mesh=mesh,
        in_specs=(
            P("view", "tok", None),
            P("view", "tok", None),
            P("view", "tok", None),
            P("view", None),
            P("view", "tok", None),
            P(),
            P(),
            P(),
            P(),
        ),
        out_specs=(P("view", "tok", None), P("view", "tok", None)),
        check_vma=False,
    )
```

```python
import math

import jax
import jax.numpy as jnp
from jax import lax
from jax.experimental import pallas as pl
from jax.experimental.pallas import tpu as pltpu
from jax.sharding import PartitionSpec as P

MESH = pl.DeviceIdType.MESH
BF = jnp.bfloat16
F32 = jnp.float32

EPSILON = 1e-06
NEGATIVE = -1e30
START_MAX = -3e38
HD = 64
LANES = 2 * HD
Z = 8
HEADS = 16
TOKS = 16
MY_ROWS = 32
HALF = MY_ROWS // 2
WIDTH = HEADS * HD
ROWS = TOKS * MY_ROWS
VIEWS = 2 * Z
SUB = 4
PIECE = ROWS // SUB
TWICE = 2
EXP2_SCALE = HD ** (-0.5) * math.log2(math.e)


def ring_distance(offset):
    return min(offset % 4, -offset % 4)


CHIP_ORDER = sorted(
    ((dx, dy) for dy in range(4) for dx in range(4)), key=lambda at: -ring_distance(at[0]) - ring_distance(at[1])
)
MEMBER_ORDER = sorted(
    ((dx, dy, dc) for dy in range(2) for dx in range(4) for dc in range(2)),
    key=lambda at: (-ring_distance(at[0]), -at[1], -at[2]),
)


def wait_bytes(like, sem):
    pltpu.make_async_copy(like, like, sem).wait()


def rows_of(ref, start, count):
    return ref.at[pl.ds(pl.multiple_of(start, count if count < 128 else 128), count), :]


def pack_keys(k_of, v_of, skv):
    low = lax.broadcasted_iota(jnp.int32, (MY_ROWS, LANES), 1) < HD
    for pair in range(HEADS // 2):
        k, v = k_of(pair), v_of(pair)
        first, second = 2 * pair * MY_ROWS, (2 * pair + 1) * MY_ROWS
        skv[first : first + MY_ROWS, :] = jnp.where(low, k, pltpu.roll(v, HD, 1)).astype(BF)
        skv[second : second + MY_ROWS, :] = jnp.where(low, pltpu.roll(k, HD, 1), v).astype(BF)


def pack_queries(q_of, sq):
    low = lax.broadcasted_iota(jnp.int32, (HALF, LANES), 1) < HD
    for pair in range(HEADS // 2):
        q = q_of(pair)
        turned = pltpu.roll(q, HD, 1)
        sq[2 * pair * HALF : (2 * pair + 1) * HALF, :] = jnp.where(low, q[:HALF], turned[HALF:]).astype(BF)
        sq[(2 * pair + 1) * HALF : (2 * pair + 2) * HALF, :] = jnp.where(low, turned[:HALF], q[HALF:]).astype(BF)


def kernel(
    nbr_hbm, q1, k1, v1, x2, w_view_out, norm_gain, w_qkv, w_out,
    feats_out, lrm_out,
    nbr, q_in, k_in, v_in, x_in, gain_in, wv, wqkv, wo,
    sqs, skvs, rqs, kvs, sos, ros,
    normed, mask_out, mask_in, qb, scores_a, scores_b, top_a, top_b, peak, acc,
    load_sem, weight_sem, a2a_send, a2a_q, a2a_kv, ring_send, ring_recv, pair_send, pair_recv, back_send, back_recv, mask_sem,
):
    view = lax.axis_index("view")
    tok = lax.axis_index("tok")
    z, y_hi = view // 2, view % 2
    core = tok % 2
    x, y_lo = tok // 2 % 4, tok // 8
    y = y_hi * 2 + y_lo
    my_head = y * 4 + x
    my_view = z * 2 + core
    at_home = core == y_hi
    right = (z + 1) % Z * 2 + y_hi
    left = (z + Z - 1) % Z * 2 + y_hi
    partner = tok + 1 - 2 * core

    loads = [
        pltpu.make_async_copy(src, dst, load_sem.at[i])
        for i, (src, dst) in enumerate(
            ((k1.at[0], k_in), (v1.at[0], v_in), (q1.at[0], q_in), (nbr_hbm, nbr), (x2.at[0], x_in), (norm_gain, gain_in))
        )
    ]
    weights = [
        pltpu.make_async_copy(src, dst, weight_sem.at[i])
        for i, (src, dst) in enumerate(((w_view_out, wv), (w_qkv, wqkv), (w_out, wo)))
    ]
    for copy in loads:
        copy.start()

    def head_device(head):
        return (z * 2 + head // 8, head // 4 % 2 * 8 + head % 4 * 2 + y_hi)

    def row_device(member):
        return (my_view, member)

    barrier = pltpu.get_barrier_semaphore()

    def greet(i, _):
        head_view, head_tok = head_device(i)

        @pl.when(jnp.logical_or(head_view != view, head_tok != tok))
        def _():
            pl.semaphore_signal(barrier, inc=1, device_id=(head_view, head_tok), device_id_type=MESH)

        @pl.when(jnp.logical_or(my_view != view, i != tok))
        def _():
            pl.semaphore_signal(barrier, inc=1, device_id=(my_view, i), device_id_type=MESH)

        return 0

    lax.fori_loop(0, TOKS, greet, 0)
    pl.semaphore_signal(barrier, inc=1, device_id=(right, tok), device_id_type=MESH)
    pl.semaphore_signal(barrier, inc=1, device_id=(left, tok), device_id_type=MESH)
    pl.semaphore_signal(barrier, inc=1, device_id=(view, partner), device_id_type=MESH)
    pl.semaphore_signal(barrier, inc=1, device_id=(right, partner), device_id_type=MESH)
    pl.semaphore_signal(barrier, inc=1, device_id=(left, partner), device_id_type=MESH)

    for copy in weights:
        copy.start()

    lane = lax.broadcasted_iota(jnp.int32, (1, LANES), 1)
    low_ones = jnp.where(lane < HD, 1.0, 0.0).astype(BF)
    high_ones = jnp.where(lane < HD, 0.0, 1.0).astype(BF)

    def spread(src_of, dst, device_of, send_sem, recv_sem):
        def remote(i):
            pltpu.make_async_remote_copy(
                src_ref=src_of(i),
                dst_ref=dst,
                send_sem=send_sem,
                recv_sem=recv_sem,
                device_id=device_of(i),
                device_id_type=MESH,
            ).start()

        for i in range(TOKS - 1):
            remote(i)

        @pl.when(at_home)
        def _():
            pltpu.make_async_copy(src_of(TOKS - 1), dst, recv_sem).start()

        @pl.when(jnp.logical_not(at_home))
        def _():
            remote(TOKS - 1)

    def nth_head(i):
        dx, dy = CHIP_ORDER[i]
        return (y + dy) % 4 * 4 + (x + dx) % 4

    def nth_member(i):
        dx, dy, dc = MEMBER_ORDER[i]
        return (y_lo + dy) % 2 * 8 + (x + dx) % 4 * 2 + (core + dc) % 2

    def send_keys(stage, skv, kv):
        spread(
            lambda i: rows_of(skv, nth_head(i) * MY_ROWS, MY_ROWS),
            rows_of(kv, view * ROWS + tok * MY_ROWS, MY_ROWS),
            lambda i: head_device(nth_head(i)),
            a2a_send.at[stage, 0],
            a2a_kv.at[stage, tok * MY_ROWS // PIECE],
        )

    def send_queries(stage, sq, rq):
        spread(
            lambda i: rows_of(sq, nth_head(i) * HALF, HALF),
            rows_of(rq, tok * HALF, HALF),
            lambda i: head_device(nth_head(i)),
            a2a_send.at[stage, 1],
            a2a_q.at[stage],
        )

    def sent(like, rows, sem):
        @pl.when(at_home)
        def _():
            wait_bytes(like.at[pl.ds(0, (HEADS - 1) * rows), :], sem)

        @pl.when(jnp.logical_not(at_home))
        def _():
            wait_bytes(like.at[pl.ds(0, HEADS * rows), :], sem)

    def ring_piece(stage, kv, direction, step, sub):
        from_z = (z + Z - step) % Z if direction == 0 else (z + step) % Z
        block = rows_of(kv, (from_z * 2 + core) * ROWS + sub * PIECE, PIECE)
        pltpu.make_async_remote_copy(
            src_ref=block,
            dst_ref=block,
            send_sem=ring_send.at[stage, direction],
            recv_sem=ring_recv.at[stage, direction, step * SUB + sub],
            device_id=(right if direction == 0 else left, tok),
            device_id_type=MESH,
        ).start()

    def to_partner(stage, kv, from_z, sub, slot, chip=None):
        block = rows_of(kv, (from_z * 2 + core) * ROWS + sub * PIECE, PIECE)
        pltpu.make_async_remote_copy(
            src_ref=block,
            dst_ref=block,
            send_sem=pair_send.at[stage],
            recv_sem=pair_recv.at[stage, slot],
            device_id=(view if chip is None else chip, partner),
            device_id_type=MESH,
        ).start()

    halves = (slice(0, ROWS // 2), slice(ROWS // 2, ROWS))

    def block_of(kv, which):
        return kv[pl.ds(pl.multiple_of(which * ROWS, ROWS), ROWS), :]

    def score(kv, which, scores, top):
        keys = block_of(kv, which) * low_ones + jnp.where(lane == HD + which, 1.0, 0.0).astype(BF)
        for cols in halves:
            part = lax.dot_general(
                keys, qb[cols, :], (((1,), (1,)), ((), ())), preferred_element_type=F32
            )
            scores[:, cols] = part
            top[:, cols] = jnp.max(part, axis=0, keepdims=True)

    def weigh(kv, which, scores, top):
        values = block_of(kv, which) * high_ones + low_ones
        for cols in halves:
            old = peak[:, cols]
            new = jnp.maximum(old, top[:, cols])
            factor = jnp.exp2((old - new) * EXP2_SCALE)
            weights16 = jnp.exp2((scores[:, cols] - new) * EXP2_SCALE).astype(BF)
            part = lax.dot_general(
                values, weights16, (((0,), (0,)), ((), ())), preferred_element_type=F32
            )
            acc[:, cols] = acc[:, cols] * factor + part
            peak[:, cols] = new

    def attend(stage, rq, kv):
        peak[...] = jnp.full_like(peak, START_MAX)
        acc[...] = jnp.zeros_like(acc)
        for sub in range(SUB):
            wait_bytes(rows_of(kv, my_view * ROWS + sub * PIECE, PIECE), a2a_kv.at[stage, sub])
            ring_piece(stage, kv, 0, 0, sub)
            ring_piece(stage, kv, 1, 0, sub)
        for sub in range(SUB):
            to_partner(stage, kv, z, sub, 0)
        wait_bytes(rq, a2a_q.at[stage])

        @pl.when(stage == 0)
        def _():
            wait_bytes(mask_in, mask_sem.at[1])

        extra = jnp.where(stage == 0, mask_in[0:1, :].astype(F32), 0.0)
        both = rq[...].astype(F32)
        qb[halves[0], :] = jnp.where(lane < HD, both, extra).astype(BF)
        qb[halves[1], :] = jnp.where(lane < HD, pltpu.roll(both, HD, 1), extra).astype(BF)

        def piece_of(step, sub, direction):
            from_z = (z + Z - step) % Z if direction == 0 else (z + step) % Z
            block = rows_of(kv, (from_z * 2 + core) * ROWS + sub * PIECE, PIECE)
            wait_bytes(block, ring_recv.at[stage, direction, (step - 1) * SUB + sub])
            return from_z

        def pieces(step, sub):
            right_z = piece_of(step, sub, 0)

            @pl.when(jnp.logical_or(step < Z // 2 - 1, sub < SUB // 2))
            def _():
                ring_piece(stage, kv, 0, step, sub)

            left_z = piece_of(step, sub, 1)

            @pl.when(jnp.logical_or(step < Z // 2 - 1, sub >= SUB // 2))
            def _():
                ring_piece(stage, kv, 1, step, sub)

            for direction, from_z, chip in ((0, right_z, right), (1, left_z, left)):
                end = SUB // 2 * (direction + 1)

                @pl.when(jnp.logical_and(step == Z // 2 - 1, jnp.logical_and(sub >= end - TWICE, sub < end)))
                def _():
                    to_partner(stage, kv, from_z, sub, Z - 1, chip)

            to_partner(stage, kv, right_z, sub, 2 * step - 1)
            to_partner(stage, kv, left_z, sub, 2 * step)

        def last_pieces(sub):
            for direction, piece in ((0, sub), (1, SUB // 2 + sub)):
                from_z = piece_of(Z // 2, piece, direction)
                if sub < SUB // 2 - TWICE:
                    to_partner(stage, kv, from_z, piece, Z - 1)

        def view_of(chip_z, whose):
            return chip_z * 2 + core + whose * (1 - 2 * core)

        def from_partner(which, slot):
            wait_bytes(rows_of(kv, which * ROWS, ROWS), pair_recv.at[stage, slot])

        a, b = (scores_a, top_a), (scores_b, top_b)
        pieces(1, 0)
        score(kv, view_of(z, 0), *a)
        pieces(1, 1)
        from_partner(view_of(z, 1), 0)
        score(kv, view_of(z, 1), *b)
        weigh(kv, view_of(z, 0), *a)
        pieces(1, 2)
        pieces(1, 3)

        def two_blocks(behind, whose, before, ahead):
            right_view = view_of((z + Z - behind) % Z, whose)
            left_view = view_of((z + behind) % Z, whose)
            ahead(0)

            @pl.when(whose == 1)
            def _():
                from_partner(right_view, 2 * behind - 1)
                from_partner(left_view, 2 * behind)

            score(kv, right_view, *a)
            weigh(kv, before, *b)
            ahead(1)
            score(kv, left_view, *b)
            weigh(kv, right_view, *a)
            return left_view

        def middle(i, before):
            behind, whose = i // 2 + 1, i % 2
            return two_blocks(behind, whose, before, lambda j: pieces(behind + 1, whose * 2 + j))

        before = lax.fori_loop(0, Z - 4, middle, view_of(z, 1))
        far = (z + Z // 2) % Z

        def final(whose, before):
            return two_blocks(Z // 2 - 1, whose, before, lambda j: None)

        before = lax.fori_loop(0, 2, final, before)
        weigh(kv, before, *b)
        last_pieces(0)
        last_pieces(1)
        score(kv, view_of(far, 0), *a)
        from_partner(view_of(far, 1), Z - 1)
        score(kv, view_of(far, 1), *b)
        weigh(kv, view_of(far, 0), *a)
        weigh(kv, view_of(far, 1), *b)

    def ring_sent(stage, kv):
        for direction in range(2):
            wait_bytes(kv.at[pl.ds(0, ((Z // 2 - 1) * SUB + SUB // 2) * PIECE), :], ring_send.at[stage, direction])
        wait_bytes(kv.at[pl.ds(0, Z * ROWS), :], pair_send.at[stage])

    def send_back(stage, so, ro):
        first, second = (acc[HD:, cols] * (1.0 / acc[0:1, cols]) for cols in halves)
        so[...] = jnp.transpose(jnp.concatenate([first, second], axis=0)).astype(BF)

        spread(
            lambda i: rows_of(so, nth_member(i) * HALF, HALF),
            rows_of(ro, my_head * HALF, HALF),
            lambda i: (my_view, nth_member(i)),
            back_send.at[stage],
            back_recv.at[stage],
        )
        wait_bytes(ro, back_recv.at[stage])

    def side_by_side(ro):
        low = lax.broadcasted_iota(jnp.int32, (HALF, LANES), 1) < HD
        parts = []
        for pair in range(HEADS // 2):
            first = ro[2 * pair * HALF : (2 * pair + 1) * HALF, :].astype(F32)
            second = ro[(2 * pair + 1) * HALF : (2 * pair + 2) * HALF, :].astype(F32)
            early = jnp.where(low, first, pltpu.roll(second, HD, 1))
            late = jnp.where(low, pltpu.roll(first, HD, 1), second)
            parts.append(jnp.concatenate([early, late], axis=0))
        return jnp.concatenate(parts, axis=1)

    def unit(values):
        return values * lax.rsqrt(jnp.mean(values * values, axis=-1, keepdims=True) + EPSILON)

    def cut(ref):
        return lambda pair: ref[:, pair * LANES : (pair + 1) * LANES].astype(F32)

    def cut_value(value):
        return lambda pair: value[:, pair * LANES : (pair + 1) * LANES]

    def project(part):
        return jnp.dot(
            normed[...], wqkv[:, part * WIDTH : (part + 1) * WIDTH], preferred_element_type=F32
        )

    for copy in loads[:2]:
        copy.wait()
    pack_keys(cut(k_in), cut(v_in), skvs.at[0])
    pl.semaphore_wait(barrier, jnp.where(at_home, 2 * TOKS + 3, 2 * TOKS + 5))

    def attention(stage, _):
        sq, skv, rq, kv, so, ro = (ref.at[stage] for ref in (sqs, skvs, rqs, kvs, sos, ros))
        send_keys(stage, skv, kv)

        @pl.when(stage == 0)
        def _():
            for copy in loads[2:4]:
                copy.wait()
            pack_queries(cut(q_in), sq)
            lanes = lax.broadcasted_iota(jnp.int32, mask_out.shape, 1)
            wanted = lanes == HD + view
            for i in range(nbr.shape[1]):
                wanted = jnp.logical_or(wanted, lanes == HD + nbr[0, i])
            mask_out[...] = jnp.where(jnp.logical_or(wanted, lanes >= HD + VIEWS), 0.0, NEGATIVE).astype(BF)

            @pl.when(at_home)
            def _():
                pltpu.make_async_copy(mask_out, mask_in, mask_sem.at[1]).start()

            @pl.when(jnp.logical_not(at_home))
            def _():
                pltpu.make_async_remote_copy(
                    src_ref=mask_out,
                    dst_ref=mask_in,
                    send_sem=mask_sem.at[0],
                    recv_sem=mask_sem.at[1],
                    device_id=(my_view, tok - core + y_hi),
                    device_id_type=MESH,
                ).start()

        @pl.when(stage == 1)
        def _():
            pack_queries(cut_value(project(0)), sq)

        send_queries(stage, sq, rq)
        attend(stage, rq, kv)
        send_back(stage, so, ro)
        rows = unit(side_by_side(ro))

        @pl.when(stage == 0)
        def _():
            feats_out[0] = rows
            for copy in loads[4:]:
                copy.wait()
            weights[0].wait()
            hidden = x_in[...].astype(F32) + jnp.dot(rows.astype(BF), wv[...], preferred_element_type=F32)
            normed[...] = (unit(hidden) * gain_in[...]).astype(BF)
            weights[1].wait()
            pack_keys(cut_value(project(1)), cut_value(project(2)), skvs.at[1])

        @pl.when(stage == 1)
        def _():
            weights[2].wait()
            lrm_out[0] = jnp.dot(rows.astype(BF), wo[...], preferred_element_type=F32)

        return 0

    lax.fori_loop(0, 2, attention, 0)

    def finish(stage, _):
        sent(skvs.at[stage], MY_ROWS, a2a_send.at[stage, 0])
        sent(sqs.at[stage], HALF, a2a_send.at[stage, 1])
        ring_sent(stage, kvs.at[stage])
        sent(sos.at[stage], HALF, back_send.at[stage])
        return 0

    lax.fori_loop(0, 2, finish, 0)

    @pl.when(jnp.logical_not(at_home))
    def _():
        wait_bytes(mask_out, mask_sem.at[0])


def per_device(q1, k1, v1, nbr, x2, w_view_out, norm_gain, w_qkv, w_out):
    anywhere = pl.BlockSpec(memory_space=pl.ANY)
    dma = pltpu.SemaphoreType.DMA
    stage_buffers = [
        pltpu.VMEM((2, HEADS * HALF, LANES), BF),
        pltpu.VMEM((2, HEADS * MY_ROWS, LANES), BF),
        pltpu.VMEM((2, TOKS * HALF, LANES), BF),
        pltpu.VMEM((2, VIEWS * ROWS, LANES), BF),
        pltpu.VMEM((2, TOKS * HALF, LANES), BF),
        pltpu.VMEM((2, HEADS * HALF, LANES), BF),
        pltpu.VMEM((MY_ROWS, WIDTH), BF),
    ]
    return tuple(pl.pallas_call(
        kernel,
        out_shape=(
            pltpu.VMEM((1, MY_ROWS, WIDTH), F32),
            pltpu.VMEM((1, MY_ROWS, WIDTH), F32),
        ),
        in_specs=[anywhere] * 9,
        out_specs=(pl.BlockSpec(memory_space=pltpu.VMEM),) * 2,
        scratch_shapes=[pltpu.SMEM((1, 7), jnp.int32)]
        + [pltpu.VMEM((MY_ROWS, WIDTH), BF)] * 4
        + [
            pltpu.VMEM((1, WIDTH), F32),
            pltpu.VMEM((WIDTH, WIDTH), BF),
            pltpu.VMEM((WIDTH, 3 * WIDTH), BF),
            pltpu.VMEM((WIDTH, WIDTH), BF),
        ]
        + stage_buffers
        + [
            pltpu.VMEM((HALF, LANES), BF),
            pltpu.VMEM((HALF, LANES), BF),
            pltpu.VMEM((ROWS, LANES), BF),
            pltpu.VMEM((ROWS, ROWS), F32),
            pltpu.VMEM((ROWS, ROWS), F32),
            pltpu.VMEM((1, ROWS), F32),
            pltpu.VMEM((1, ROWS), F32),
            pltpu.VMEM((1, ROWS), F32),
            pltpu.VMEM((LANES, ROWS), F32),
            dma((6,)),
            dma((3,)),
            dma((2, 2)),
            dma((2,)),
            dma((2, SUB)),
            dma((2, 2)),
            dma((2, 2, Z // 2 * SUB)),
            dma((2,)),
            dma((2, Z)),
            dma((2,)),
            dma((2,)),
            dma((2,)),
        ],
        compiler_params=pltpu.CompilerParams(
            collective_id=0, has_side_effects=True, vmem_limit_bytes=56 * 1024 * 1024
        ),
    )(nbr, q1, k1, v1, x2, w_view_out, norm_gain.reshape(1, -1), w_qkv, w_out))


def solution(mesh):
    return jax.shard_map(
        per_device,
        mesh=mesh,
        in_specs=(
            P("view", "tok", None),
            P("view", "tok", None),
            P("view", "tok", None),
            P("view", None),
            P("view", "tok", None),
            P(),
            P(),
            P(),
            P(),
        ),
        out_specs=(P("view", "tok", None), P("view", "tok", None)),
        check_vma=False,
    )
```
